32 devices in a mesh: grp: 1, seq: 8 (over z, y), head: 4 (over x, core).
Axes of the slice: x: 2, y: 2, z: 4, core: 2. Of those that a mesh axis runs over, the one named last changes fastest.
Arguments:
- ssm_values: bfloat16 [2048, 4096], P(('grp', 'seq'), 'head'), may hold values from -6 to 6
- ssm_gate: bfloat16 [2048, 4096], P(('grp', 'seq'), 'head'), may hold values from -6 to 6
- write_proj: bfloat16 [2048, 1024], P(('grp', 'seq'), 'head'), may hold values from -2.5 to 2.5
- read_proj: bfloat16 [2048, 1024], P(('grp', 'seq'), 'head'), may hold values from -2.5 to 2.5
- step_size: float32 [2048, 64], P(('grp', 'seq'), 'head'), may hold values from 0.003125 to 0.2
- decay_power: int32 [64], P('head'), may hold values from 0 to 15
- skip_gain: float32 [64], P('head'), may hold values from 0.5 to 1.5
- norm_gain: float32 [4096], P('head'), may hold values from 0.1 to 1.9
- out_weight: bfloat16 [4096, 2688], P('head', 'seq'), may hold values from -0.09375 to 0.09375
- residual: bfloat16 [2048, 2688], P(('grp', 'seq', 'head')), may hold values from -6 to 6
- expert_norm: float32 [2688], replicated, may hold values from 0.1 to 1.9
- router_weight: bfloat16 [2688, 16], replicated, may hold values from -0.125 to 0.125
- expert_index: int32 [2048, 6], P(('grp', 'seq', 'head')), may hold values from 0 to 15, all different within a row; in each aligned block of 64 rows (0 to 63, 64 to 127, ...) at most 32 rows name the same one
- up_weight: bfloat16 [32, 2688, 928], P(('seq', 'head')), may hold values from -0.125 to 0.125
- down_weight: bfloat16 [32, 928, 2688], P(('seq', 'head')), may hold values from -0.125 to 0.125
Outputs:
- layer_out: bfloat16 [2048, 2688], P(('grp', 'seq', 'head'))
The draws below stay inside these ranges and needn't reach their ends.
Inputs may be any that keep to these rules, and one draw needn't show every extreme that they name: `expert_index`: each row names 6 different experts. In the rows of one device (aligned blocks of 64 rows) no expert is named more than 32 times, a bound that some block reaches.
All inputs are finite; a program needn't handle non-finite values.
Results may differ from the reference program's by a relative error of at most 0.019.
Values may be sent and summed in bfloat16 or wider, within the bound.
No kernel may reach another device: no remote copies, remote signals or barrier semaphores. Data moves between devices by JAX's collectives and lax.ppermute only.
A program may use at most 64 MiB of HBM per device.

```python
import math
import jax
import jax.numpy as jnp
import numpy as np
from jax import lax

D = 2688
FF = 1856
HEADS = 64
HEAD_DIM = 64
STATE = 128
GROUPS = 8
TOP = 6
BLOCK_LEN = 256
TOK_DEV = 256
TOKENS = 2048
EXPERTS = 16
CAP = 32
N_HEAD = 4


def draw_step_size(key, part):
    base_key = jax.random.fold_in(key, 11)
    factor_key = jax.random.fold_in(key, 23)
    base = jnp.exp(jax.random.uniform(base_key, (TOKENS, HEADS), jnp.float32, math.log(0.0125), math.log(0.05)))
    shards = TOKENS // TOK_DEV
    factor = jnp.exp(jax.random.uniform(factor_key, (shards, 1, HEADS), jnp.float32, math.log(0.25), math.log(4.0)))
    return (base.reshape(shards, TOK_DEV, HEADS) * factor).reshape(TOKENS, HEADS)


def set_ends(values, stream_key, smallest, top_value):
    index_at = [jax.random.randint(jax.random.fold_in(stream_key, axis), (), 0, length) for axis, length in enumerate(values.shape)]
    longest = values.shape.index(max(values.shape))
    beside = index_at[:longest] + [(index_at[longest] + 1) % values.shape[longest]] + index_at[longest + 1:]
    return values.at[tuple(index_at)].set(smallest).at[tuple(beside)].set(top_value)


def levels(own_key, dims, split, least, top_value):
    loudness = 1.0
    for axis_at, parts in split:
        steps = jax.random.uniform(jax.random.fold_in(jax.random.fold_in(own_key, 6), axis_at), (parts,), jnp.float32, least / len(split), top_value / len(split))
        loudness = loudness * jnp.repeat(jnp.exp(steps), dims[axis_at] // parts).reshape((-1,) + (1,) * (len(dims) - 1 - axis_at))
    return loudness


def assign_block(key, own, number, rows, amount, top, reach, slope):
    order = jax.random.permutation(key, amount)
    crowded, common = load_shares(amount, rows * top, reach, slope, True), load_shares(amount, rows * top, reach, slope, False)
    places = jnp.arange(amount)

    def named(sizes, rotation):
        used = int((sizes > 0).sum())
        fixed = max(1, used // 4)
        shifted = fixed + (places - fixed + rotation * (used - fixed)) % max(1, amount - fixed)
        return jnp.zeros((amount,), jnp.int32).at[order[jnp.where(places < fixed, places, shifted)]].set(jnp.asarray(sizes, jnp.int32))

    sizes = jnp.where(number % 4 == 0, named(crowded, number // 4), named(common, number - number // 4 - 1))
    mixed = jax.random.permutation(jax.random.fold_in(own, 3), amount)
    giver, receiver = mixed[0:amount // 2 * 2:2], mixed[1:amount // 2 * 2:2]
    margin = jnp.minimum(sizes[giver] - 1, reach - sizes[receiver]) // 2
    margin = jnp.where((giver == order[0]) | (receiver == order[0]) | (sizes[receiver] == 0), 0, jnp.maximum(margin, 0))
    shifted = jax.random.randint(jax.random.fold_in(own, 4), (amount // 2,), 0, 1 << 20) % (margin + 1)
    sizes = sizes.at[giver].add(-shifted).at[receiver].add(shifted)
    items = jnp.searchsorted(jnp.cumsum(sizes), jnp.arange(rows * top), side="right").astype(jnp.int32)
    table = items.reshape(top, rows).T
    table = table[jax.random.permutation(jax.random.fold_in(own, 1), rows)]
    rotation = jax.random.randint(jax.random.fold_in(own, 2), (rows, 1), 0, top)
    return jnp.take_along_axis(table, (jnp.arange(top)[None, :] + rotation) % top, axis=1)


def load_shares(number_of, total, reach, skew, full):
    weights = [(1 << 20) // math.isqrt(rank ** skew) + 1 for rank in range(1, number_of + 1)]
    largest = reach if full else min(reach, max(-(-total // number_of), total * weights[0] // sum(weights)))
    least = 1 if total - largest >= number_of - 1 else 0
    holding, spare = [largest] + [least] * (number_of - 1), total - largest - least * (number_of - 1)
    while spare > 0:
        movable = [i for i in range(1, number_of) if holding[i] < largest] or [i for i in range(1, number_of) if holding[i] < reach]
        mass, left = sum([weights[i] for i in movable]), spare
        for i in movable:
            extra = min(reach - holding[i], max(1, left * weights[i] // mass), spare)
            holding[i] = holding[i] + extra
            spare = spare - extra
    return np.array(holding)


def normal_values(stream_key, dims, scale, limit, cuts=(), kind=jnp.bfloat16):
    level = levels(stream_key, dims, cuts, -0.22, 0.18) if cuts else 1.0
    values = jax.random.normal(stream_key, dims, jnp.float32) * scale * level
    return jnp.minimum(jnp.maximum(values, -limit), limit).astype(kind)


def setup_inputs(seed: int = 0, part: int = 0) -> dict:
    seeds = jax.random.split(jax.random.key(seed), 16)
    own_keys = jax.random.split(jax.random.fold_in(seeds[15], part), 16)
    ssm_values = normal_values(own_keys[0], (TOKENS, HEADS * HEAD_DIM), 1.0, 6.0, ((0, 8), (1, 4)))
    ssm_gate = normal_values(own_keys[1], (TOKENS, HEADS * HEAD_DIM), 1.0, 6.0, ((0, 8), (1, 4)))
    write_proj = normal_values(own_keys[2], (TOKENS, GROUPS * STATE), 0.35, 2.5, ((0, 8), (1, 4)))
    read_proj = normal_values(own_keys[3], (TOKENS, GROUPS * STATE), 0.35, 2.5, ((0, 8), (1, 4)))
    step_size = draw_step_size(jax.random.fold_in(jax.random.fold_in(seeds[15], part), 71), part)
    decay_power = set_ends(jax.random.randint(seeds[5], (HEADS,), 0, 16), jax.random.fold_in(seeds[5], 1), 0, 15).astype(jnp.int32)
    skip_gain = jnp.clip(0.5 + 1.0 * jax.random.uniform(seeds[6], (HEADS,), jnp.float32) ** levels(seeds[6], (HEADS,), ((0, 4),), -0.2, 0.2), 0.5, 1.5)
    norm_gain = jnp.clip(1.0 + 0.18 * jax.random.normal(seeds[7], (HEADS * HEAD_DIM,), jnp.float32), 0.1, 1.9)
    out_weight = normal_values(seeds[8], (HEADS * HEAD_DIM, D), (HEADS * HEAD_DIM) ** -0.5, 0.09375, ((0, 4), (1, 8)))
    residual = normal_values(own_keys[9], (TOKENS, D), 1.0, 6.0, ((0, 32),))
    expert_norm = jnp.clip(1.0 + 0.18 * jax.random.normal(seeds[10], (D,), jnp.float32), 0.1, 1.9)
    router_weight = normal_values(seeds[11], (D, EXPERTS), D ** -0.5, 0.125)
    expert_index_keys = jax.random.split(jax.random.fold_in(own_keys[12], 1), TOKENS // (TOK_DEV // N_HEAD))
    expert_index_turns = jax.random.permutation(jax.random.fold_in(own_keys[12], 3), TOKENS // (TOK_DEV // N_HEAD))
    expert_index = jax.vmap(lambda own, number: assign_block(jax.random.fold_in(own_keys[12], 2), own, number, TOK_DEV // N_HEAD, EXPERTS, TOP, CAP, 2))(expert_index_keys, expert_index_turns).reshape((TOKENS, TOP))
    up_weight = normal_values(seeds[13], (2 * EXPERTS, D, FF // 2), D ** -0.5, 0.125, ((0, 32),))
    down_weight = normal_values(seeds[14], (2 * EXPERTS, FF // 2, D), FF ** -0.5, 0.125, ((0, 32),))
    return {"ssm_values": ssm_values, "ssm_gate": ssm_gate, "write_proj": write_proj, "read_proj": read_proj, "step_size": step_size, "decay_power": decay_power, "skip_gain": skip_gain, "norm_gain": norm_gain, "out_weight": out_weight, "residual": residual, "expert_norm": expert_norm, "router_weight": router_weight, "expert_index": expert_index, "up_weight": up_weight, "down_weight": down_weight}


EPSILON = 1e-05
ROUTE_SCALE = 2.5

def rounded(value):
    return lax.optimization_barrier(value.astype(jnp.bfloat16)).astype(jnp.float32)

def reference(ssm_values, ssm_gate, write_proj, read_proj, step_size, decay_power, skip_gain, norm_gain, out_weight, residual, expert_norm, router_weight, expert_index, up_weight, down_weight):
    per_group = HEADS // GROUPS
    decay_rates = jnp.exp2(-decay_power.astype(jnp.float32))
    blocks = TOKENS // BLOCK_LEN
    block_values = ssm_values.reshape(blocks, BLOCK_LEN, HEADS, HEAD_DIM)
    block_steps = step_size.reshape(blocks, BLOCK_LEN, HEADS)
    block_write = write_proj.reshape(blocks, BLOCK_LEN, GROUPS, STATE)
    block_read = read_proj.reshape(blocks, BLOCK_LEN, GROUPS, STATE)
    causal = jnp.tril(jnp.ones((BLOCK_LEN, BLOCK_LEN), dtype=bool))

    def advance(carry_state, pieces):
        values_in, steps_in, write_in, read_in = pieces
        log_decay = -steps_in * decay_rates[None, :]
        cumulative = jnp.cumsum(log_decay, axis=0)
        scores = jnp.einsum('tgn,sgn->gts', read_in.astype(jnp.float32), write_in.astype(jnp.float32))
        scores = jnp.repeat(scores, per_group, axis=0)
        decays = jnp.exp(cumulative.T[:, :, None] - cumulative.T[:, None, :])
        mixing = rounded(jnp.where(causal[None], scores * decays * steps_in.T[:, None, :], 0.0))
        inner_out = jnp.einsum('hts,shp->thp', mixing, values_in.astype(jnp.float32))
        block_total = cumulative[-1]
        weighted = rounded(values_in.astype(jnp.float32) * (jnp.exp(block_total[None, :] - cumulative) * steps_in)[:, :, None])
        write_heads = jnp.repeat(write_in, per_group, axis=1).astype(jnp.float32)
        read_heads = jnp.repeat(read_in, per_group, axis=1).astype(jnp.float32)
        fresh_state = jnp.einsum('shp,shn->hpn', weighted, write_heads)
        carried = jnp.einsum('thn,hpn->thp', read_heads, rounded(carry_state)) * jnp.exp(cumulative)[:, :, None]
        new_state = jnp.exp(block_total)[:, None, None] * carry_state + fresh_state
        return (new_state, inner_out + carried)
    zero_state = jnp.zeros((HEADS, HEAD_DIM, STATE), jnp.float32)
    final_state, outputs = lax.scan(advance, zero_state, (block_values, block_steps, block_write, block_read))
    values_all = ssm_values.reshape(TOKENS, HEADS, HEAD_DIM).astype(jnp.float32)
    ssm_out = outputs.reshape(TOKENS, HEADS, HEAD_DIM) + skip_gain[None, :, None] * values_all
    gate_vals = ssm_gate.reshape(TOKENS, HEADS, HEAD_DIM).astype(jnp.float32)
    gated = (ssm_out * jax.nn.silu(gate_vals)).reshape(TOKENS, GROUPS, per_group * HEAD_DIM)
    inv_rms = lax.rsqrt(lax.optimization_barrier(jnp.mean(gated * gated, axis=-1, keepdims=True)) + EPSILON)
    normed = ((gated * inv_rms).reshape(TOKENS, HEADS * HEAD_DIM) * norm_gain[None, :]).astype(jnp.bfloat16)
    mixed_out = jnp.dot(normed, out_weight, preferred_element_type=jnp.float32)
    hidden = residual.astype(jnp.float32) + mixed_out
    inputs = (hidden * lax.rsqrt(lax.optimization_barrier(jnp.mean(hidden * hidden, axis=-1, keepdims=True)) + EPSILON) * expert_norm[None, :]).astype(jnp.bfloat16)
    logits = jnp.dot(inputs, router_weight, preferred_element_type=jnp.float32)
    picked = jnp.take_along_axis(logits, expert_index, axis=1)
    probability = jax.nn.sigmoid(picked)
    shares = ROUTE_SCALE * probability / lax.optimization_barrier(jnp.sum(probability, axis=1, keepdims=True))
    rows_dev = TOK_DEV // N_HEAD
    count_blocks = TOKENS // rows_dev
    expert_hits = (expert_index[:, :, None] == jnp.arange(EXPERTS, dtype=jnp.int32)[None, None, :]).astype(jnp.int32)
    flat_hits = expert_hits.reshape(count_blocks, rows_dev * TOP, EXPERTS)
    before = jnp.cumsum(flat_hits, axis=1) - flat_hits
    slot_index = lax.optimization_barrier(jnp.sum(before * flat_hits, axis=-1)).reshape(TOKENS * TOP)
    expert_flat = expert_index.reshape(TOKENS * TOP)
    token_ids = jnp.repeat(jnp.arange(TOKENS, dtype=jnp.int32), TOP)
    column = token_ids // rows_dev * CAP + slot_index
    row_table = jnp.full((EXPERTS, count_blocks * CAP), TOKENS, jnp.int32).at[expert_flat, column].set(token_ids)
    share_table = jnp.zeros((EXPERTS, count_blocks * CAP), jnp.float32).at[expert_flat, column].set(shares.reshape(TOKENS * TOP))
    padded = jnp.concatenate([inputs, jnp.zeros((1, D), jnp.bfloat16)], axis=0)
    up_pairs = up_weight.reshape(EXPERTS, 2, D, FF // 2)
    down_pairs = down_weight.reshape(EXPERTS, 2, FF // 2, D)

    def expert(totals, pieces):
        up_pair, down_pair, row_ids, share_row = pieces
        chosen = padded[row_ids]
        half_outs = []
        for half_index in range(2):
            activation = jnp.dot(chosen, up_pair[half_index], preferred_element_type=jnp.float32)
            activation = jnp.maximum(activation, 0.0)
            activation = (activation * activation).astype(jnp.bfloat16)
            half_outs.append(rounded(jnp.dot(activation, down_pair[half_index], preferred_element_type=jnp.float32)))
        result = rounded(half_outs[0] + half_outs[1])
        totals = totals.at[row_ids].add(share_row[:, None] * result)
        return (totals, None)
    initial = jnp.zeros((TOKENS + 1, D), jnp.float32)
    totals, unused = lax.scan(expert, initial, (up_pairs, down_pairs, row_table, share_table))
    return (hidden + totals[:TOKENS]).astype(jnp.bfloat16)
```

```python
import jax
import jax.numpy as jnp
from jax import lax
from jax.sharding import PartitionSpec as P

HEADS = 64
HEAD_DIM = 64
STATE = 128
GROUPS = 8
TOP = 6
BLOCK_LEN = 256


EPSILON = 1e-05
ROUTE_SCALE = 2.5


def seq_ring(size):
    return list(range(0, size, 2)) + list(range(1, size, 2))[::-1]


def shift(x, axis, order, step):
    size = len(order)
    return lax.ppermute(x, axis, [(order[i], order[(i + step) % size]) for i in range(size)])


def pick(parts, index):
    return lax.dynamic_index_in_dim(parts, index, 0, keepdims=False)


def packed(state, decay):
    high = decay.astype(jnp.bfloat16)
    low = (decay - high.astype(jnp.float32)).astype(jnp.bfloat16)
    rows = jnp.zeros((16, STATE), jnp.bfloat16)
    rows = rows.at[0, : decay.shape[0]].set(high).at[1, : decay.shape[0]].set(low)
    return jnp.concatenate([state.reshape(-1, STATE).astype(jnp.bfloat16), rows], axis=0)


def unpacked(block, heads):
    rows = heads * HEAD_DIM
    state = block[:rows].astype(jnp.float32).reshape(heads, HEAD_DIM, STATE)
    decay = block[rows, :heads].astype(jnp.float32) + block[rows + 1, :heads].astype(jnp.float32)
    return state, decay


def entering(decay, state, axis):
    size, mine = lax.axis_size(axis), lax.axis_index(axis)
    half = decay.shape[0] // 2
    odd = mine % 2 == 1
    swap = [(i, i ^ 1) for i in range(size)]
    states = state.reshape(2, half, HEAD_DIM, STATE)
    decays = decay.reshape(2, half)
    side = mine % 2
    got = lax.ppermute(packed(pick(states, 1 - side), pick(decays, 1 - side)), axis, swap)
    other_state, other_decay = unpacked(got, half)
    own_state, own_decay = pick(states, side), pick(decays, side)
    first_state = jnp.where(odd, other_state, own_state)
    second_state = jnp.where(odd, own_state, other_state)
    first_decay = jnp.where(odd, other_decay, own_decay)
    second_decay = jnp.where(odd, own_decay, other_decay)
    pair = packed(
        second_decay[:, None, None] * first_state + second_state, first_decay * second_decay
    )
    before = None
    received = [
        lax.ppermute(pair, axis, [(i, i + 2 * d) for i in range(size - 2 * d)])
        for d in range(1, size // 2)
    ]
    for block in received[::-1]:
        block_state, block_decay = unpacked(block, half)
        before = (
            block_state
            if before is None
            else block_decay[:, None, None] * before + block_state
        )
    if before is None:
        before = jnp.zeros_like(first_state)
    inner = first_decay[:, None, None] * before + first_state
    mine_half = jnp.where(odd, inner, before)
    send_half = jnp.where(odd, before, inner).astype(jnp.bfloat16)
    back = lax.ppermute(send_half.reshape(-1, STATE), axis, swap)
    back = back.astype(jnp.float32).reshape(mine_half.shape)
    low = jnp.where(odd, back, mine_half)
    high = jnp.where(odd, mine_half, back)
    return jnp.concatenate([low, high], axis=0)


def ring_weights(out_weight, axis):
    size = lax.axis_size(axis)
    order = seq_ring(size)
    shard = out_weight.T
    cut = (shard.shape[0] // 2 + 15) // 16 * 16
    top, bottom = shard[:cut], shard[cut:]
    groups = [([0], [shard])]
    ahead, behind = (top, bottom), (top, bottom)
    for step in range(1, size // 2 + 1):
        if 2 * step < size:
            ahead = tuple(shift(part, axis, order, 1) for part in ahead)
            behind = tuple(shift(part, axis, order, -1) for part in behind)
            groups.append(([-step, step], [*ahead, *behind]))
        else:
            last = (shift(ahead[0], axis, order, 1), shift(behind[1], axis, order, -1))
            groups.append(([-step], [*last]))
    return groups


def head_scatter(pieces, axis):
    size, mine = lax.axis_size(axis), lax.axis_index(axis)
    stride = 1
    while stride < size:
        bit = (mine // stride) % 2
        left = pieces.shape[0] // 2
        view = pieces.reshape(left, 2, *pieces.shape[1:])
        send = lax.dynamic_index_in_dim(view, 1 - bit, 1, keepdims=False)
        keep = lax.dynamic_index_in_dim(view, bit, 1, keepdims=False)
        came = lax.ppermute(send, axis, [(i, i ^ stride) for i in range(size)])
        pieces = (keep.astype(jnp.float32) + came.astype(jnp.float32)).astype(jnp.bfloat16)
        stride *= 2
    return pieces[0]


def partner(x, axis, stride):
    return lax.ppermute(x, axis, [(i, i ^ 1 << stride) for i in range(lax.axis_size(axis))])


def expert_half(slot_rows, up_weight, down_weight):
    model_width = slot_rows.shape[-1]
    flat_rows = slot_rows.reshape(-1, model_width)
    activation = jnp.dot(flat_rows, up_weight[0], preferred_element_type=jnp.float32)
    activation = jnp.maximum(activation, 0.0)
    activation = (activation * activation).astype(jnp.bfloat16)
    output = jnp.dot(activation, down_weight[0], preferred_element_type=jnp.float32).astype(
        jnp.bfloat16
    )
    return output.reshape(slot_rows.shape)


def per_device(
    ssm_values,
    ssm_gate,
    write_proj,
    read_proj,
    step_size,
    decay_power,
    skip_gain,
    norm_gain,
    out_weight,
    residual,
    expert_norm,
    router_weight,
    expert_index,
    up_weight,
    down_weight,
):
    tokens_dev = ssm_values.shape[0]
    heads_dev = step_size.shape[1]
    per_group = HEADS // GROUPS
    groups_dev = heads_dev // per_group
    count_blocks = tokens_dev // BLOCK_LEN
    weight_groups = ring_weights(out_weight, "seq")
    decay_rates = jnp.exp2(-decay_power.astype(jnp.float32))
    values = ssm_values.reshape(count_blocks, BLOCK_LEN, heads_dev, HEAD_DIM)
    steps_all = step_size.reshape(count_blocks, BLOCK_LEN, heads_dev)
    writes = write_proj.reshape(count_blocks, BLOCK_LEN, groups_dev, STATE)
    reads = read_proj.reshape(count_blocks, BLOCK_LEN, groups_dev, STATE)
    causal = jnp.tril(jnp.ones((BLOCK_LEN, BLOCK_LEN), dtype=bool))

    def one_block(pieces):
        values_in, steps_in, write_in, read_in = pieces
        log_decay = -steps_in * decay_rates[None, :]
        cumulative = jnp.cumsum(log_decay, axis=0)
        scores = jnp.einsum("tgn,sgn->gts", read_in, write_in, preferred_element_type=jnp.float32)
        scores = jnp.repeat(scores, per_group, axis=0)
        decays = jnp.exp(cumulative.T[:, :, None] - cumulative.T[:, None, :])
        mixing = jnp.where(causal[None], scores * decays * steps_in.T[:, None, :], 0.0).astype(
            jnp.bfloat16
        )
        inner_out = jnp.einsum(
            "hts,shp->thp", mixing, values_in, preferred_element_type=jnp.float32
        )
        block_total = cumulative[-1]
        weighted = (
            values_in.astype(jnp.float32)
            * (jnp.exp(block_total[None, :] - cumulative) * steps_in)[:, :, None]
        ).astype(jnp.bfloat16)
        write_heads = jnp.repeat(write_in, per_group, axis=1)
        fresh_state = jnp.einsum(
            "shp,shn->hpn", weighted, write_heads, preferred_element_type=jnp.float32
        )
        return (inner_out, fresh_state, block_total, cumulative)

    inner_all, fresh_all, totals_blk, cumul_all = lax.map(
        one_block, (values, steps_all, writes, reads)
    )

    def summarize(carried_in, pieces):
        decay_prod, summary = carried_in
        block_total, fresh_state = pieces
        factor = jnp.exp(block_total)
        return ((decay_prod * factor, factor[:, None, None] * summary + fresh_state), None)

    zero_state = jnp.zeros((heads_dev, HEAD_DIM, STATE), jnp.float32)
    (device_decay, device_state), unused = lax.scan(
        summarize, (jnp.ones((heads_dev,), jnp.float32), zero_state), (totals_blk, fresh_all)
    )

    incoming = entering(device_decay, device_state, "seq")

    def emit_rows(carry_state, pieces):
        read_in, cumulative, block_total, fresh_state = pieces
        read_heads = jnp.repeat(read_in, per_group, axis=1)
        carried = jnp.einsum(
            "thn,hpn->thp",
            read_heads,
            carry_state.astype(jnp.bfloat16),
            preferred_element_type=jnp.float32,
        )
        carried = carried * jnp.exp(cumulative)[:, :, None]
        return (jnp.exp(block_total)[:, None, None] * carry_state + fresh_state, carried)

    final_state, carried_all = lax.scan(
        emit_rows, incoming, (reads, cumul_all, totals_blk, fresh_all)
    )
    values_flat = ssm_values.reshape(tokens_dev, heads_dev, HEAD_DIM).astype(jnp.float32)
    ssm_out = (inner_all + carried_all).reshape(tokens_dev, heads_dev, HEAD_DIM) + skip_gain[
        None, :, None
    ] * values_flat
    gate_vals = ssm_gate.reshape(tokens_dev, heads_dev, HEAD_DIM).astype(jnp.float32)
    gated = (ssm_out * jax.nn.silu(gate_vals)).reshape(tokens_dev, groups_dev, per_group * HEAD_DIM)
    inv_rms = lax.rsqrt(jnp.mean(gated * gated, axis=-1, keepdims=True) + EPSILON)
    normed = (
        (gated * inv_rms).reshape(tokens_dev, heads_dev * HEAD_DIM) * norm_gain[None, :]
    ).astype(jnp.bfloat16)
    seq_size = lax.axis_size("seq")
    head_size = lax.axis_size("head")
    rows_own = tokens_dev // head_size
    shard_width = out_weight.shape[1]
    offsets, products = [], []
    for steps, parts in weight_groups:
        rows = parts[0] if len(parts) == 1 else jnp.concatenate(parts, axis=0)
        product = lax.dot_general(
            normed, rows, (((1,), (1,)), ((), ())), preferred_element_type=jnp.float32
        ).astype(jnp.bfloat16)
        for at, step in enumerate(steps):
            offsets.append(step)
            products.append(product[:, at * shard_width : (at + 1) * shard_width])
    stacked = jnp.stack(products, axis=0).reshape(
        seq_size, head_size, rows_own, shard_width
    )
    scattered = head_scatter(stacked.transpose(1, 0, 2, 3), "head").astype(jnp.float32)
    order = seq_ring(seq_size)
    table = [[0] * seq_size for _ in range(seq_size)]
    for place, index in enumerate(order):
        for at, step in enumerate(offsets):
            table[index][order[(place + step) % seq_size]] = at
    places = jnp.asarray(table, jnp.int32)[lax.axis_index("seq")]
    mixed_out = jnp.concatenate(
        [pick(scattered, places[b]) for b in range(seq_size)], axis=1
    )
    hidden = residual.astype(jnp.float32) + mixed_out
    inputs = (
        hidden
        * lax.rsqrt(jnp.mean(hidden * hidden, axis=-1, keepdims=True) + EPSILON)
        * expert_norm[None, :]
    ).astype(jnp.bfloat16)
    logits = jnp.dot(inputs, router_weight, preferred_element_type=jnp.float32)
    experts = router_weight.shape[1]
    model_width = inputs.shape[1]
    expert_hits = expert_index[:, :, None] == jnp.arange(experts, dtype=jnp.int32)[None, None, :]
    picked = jnp.sum(jnp.where(expert_hits, logits[:, None, :], 0.0), axis=-1)
    probability = jax.nn.sigmoid(picked)
    shares = ROUTE_SCALE * probability / jnp.sum(probability, axis=1, keepdims=True)
    capacity = (
        8
        * TOP
        * tokens_dev
        // (3 * lax.axis_size("seq") * lax.axis_size("head") * lax.axis_size("head"))
    )
    flat_hits = expert_hits.astype(jnp.int32).reshape(rows_own * TOP, experts)
    before = jnp.cumsum(flat_hits, axis=0) - flat_hits
    slot_index = jnp.sum(before * flat_hits, axis=1)
    target = expert_index.reshape(rows_own * TOP) * capacity + slot_index
    placing = jnp.arange(experts * capacity, dtype=jnp.int32)[:, None] == target[None, :]
    placing = jnp.any(placing.reshape(experts * capacity, rows_own, TOP), axis=2).astype(
        jnp.bfloat16
    )
    outgoing = jnp.dot(placing, inputs, preferred_element_type=jnp.float32).astype(jnp.bfloat16)
    outgoing = outgoing.reshape(experts, capacity, model_width)
    halves = outgoing.reshape(experts, 2, capacity // 2, model_width).reshape(
        2 * experts, capacity // 2, model_width
    )
    slot_rows = lax.all_to_all(halves, ("seq", "head"), split_axis=0, concat_axis=0, tiled=True)
    other_rows = partner(slot_rows, "head", 0)
    both_rows = jnp.concatenate([slot_rows, other_rows], axis=1)
    both_parts = expert_half(both_rows, up_weight, down_weight)
    own_part = both_parts[:, : slot_rows.shape[1]]
    other_part = both_parts[:, slot_rows.shape[1] :]
    back_part = partner(other_part, "head", 0)
    summed = (own_part.astype(jnp.float32) + back_part.astype(jnp.float32)).astype(jnp.bfloat16)
    returned = lax.all_to_all(summed, ("seq", "head"), split_axis=0, concat_axis=0, tiled=True)
    results = returned.reshape(experts, 2, capacity // 2, model_width).reshape(
        experts, capacity, model_width
    )
    gathered = results.reshape(experts * capacity, model_width)[target].reshape(
        rows_own, TOP, model_width
    )
    moe_out = jnp.sum(shares[:, :, None] * gathered.astype(jnp.float32), axis=1)
    return (hidden + moe_out).astype(jnp.bfloat16)


def solution(mesh):
    return jax.shard_map(
        per_device,
        mesh=mesh,
        in_specs=(
            P(("grp", "seq"), "head"),
            P(("grp", "seq"), "head"),
            P(("grp", "seq"), "head"),
            P(("grp", "seq"), "head"),
            P(("grp", "seq"), "head"),
            P("head"),
            P("head"),
            P("head"),
            P("head", "seq"),
            P(("grp", "seq", "head"), None),
            P(),
            P(),
            P(("grp", "seq", "head"), None),
            P(("seq", "head"), None, None),
            P(("seq", "head"), None, None),
        ),
        out_specs=P(("grp", "seq", "head"), None),
        check_vma=False,
    )
```

```python
import jax
import jax.numpy as jnp
from jax import lax
from jax.sharding import PartitionSpec as P

HEADS = 64
HEAD_DIM = 64
STATE = 128
GROUPS = 8
TOP = 6
BLOCK_LEN = 256


EPSILON = 1e-05
ROUTE_SCALE = 2.5


def seq_ring(size):
    return list(range(0, size, 2)) + list(range(1, size, 2))[::-1]


def shift(x, axis, order, step):
    size = len(order)
    return lax.ppermute(x, axis, [(order[i], order[(i + step) % size]) for i in range(size)])


def pick(parts, index):
    return lax.dynamic_index_in_dim(parts, index, 0, keepdims=False)


def packed(state, decay):
    high = decay.astype(jnp.bfloat16)
    low = (decay - high.astype(jnp.float32)).astype(jnp.bfloat16)
    rows = jnp.zeros((16, STATE), jnp.bfloat16)
    rows = rows.at[0, : decay.shape[0]].set(high).at[1, : decay.shape[0]].set(low)
    return jnp.concatenate([state.reshape(-1, STATE).astype(jnp.bfloat16), rows], axis=0)


def unpacked(block, heads):
    rows = heads * HEAD_DIM
    state = block[:rows].astype(jnp.float32).reshape(heads, HEAD_DIM, STATE)
    decay = block[rows, :heads].astype(jnp.float32) + block[rows + 1, :heads].astype(jnp.float32)
    return state, decay


def entering(decay, state, axis):
    size, mine = lax.axis_size(axis), lax.axis_index(axis)
    half = decay.shape[0] // 2
    odd = mine % 2 == 1
    swap = [(i, i ^ 1) for i in range(size)]
    states = state.reshape(2, half, HEAD_DIM, STATE)
    decays = decay.reshape(2, half)
    side = mine % 2
    got = lax.ppermute(packed(pick(states, 1 - side), pick(decays, 1 - side)), axis, swap)
    other_state, other_decay = unpacked(got, half)
    own_state, own_decay = pick(states, side), pick(decays, side)
    first_state = jnp.where(odd, other_state, own_state)
    second_state = jnp.where(odd, own_state, other_state)
    first_decay = jnp.where(odd, other_decay, own_decay)
    second_decay = jnp.where(odd, own_decay, other_decay)
    pair = packed(
        second_decay[:, None, None] * first_state + second_state, first_decay * second_decay
    )
    before = None
    received = [
        lax.ppermute(pair, axis, [(i, i + 2 * d) for i in range(size - 2 * d)])
        for d in range(1, size // 2)
    ]
    for block in received[::-1]:
        block_state, block_decay = unpacked(block, half)
        before = (
            block_state
            if before is None
            else block_decay[:, None, None] * before + block_state
        )
    if before is None:
        before = jnp.zeros_like(first_state)
    inner = first_decay[:, None, None] * before + first_state
    mine_half = jnp.where(odd, inner, before)
    send_half = jnp.where(odd, before, inner).astype(jnp.bfloat16)
    back = lax.ppermute(send_half.reshape(-1, STATE), axis, swap)
    back = back.astype(jnp.float32).reshape(mine_half.shape)
    low = jnp.where(odd, back, mine_half)
    high = jnp.where(odd, mine_half, back)
    return jnp.concatenate([low, high], axis=0)


def ring_weights(out_weight, axis):
    size = lax.axis_size(axis)
    order = seq_ring(size)
    shard = out_weight.T
    cut = (shard.shape[0] // 2 + 15) // 16 * 16
    top, bottom = shard[:cut], shard[cut:]
    groups = [([0], [shard])]
    ahead, behind = (top, bottom), (top, bottom)
    for step in range(1, size // 2 + 1):
        if 2 * step < size:
            ahead = tuple(shift(part, axis, order, 1) for part in ahead)
            behind = tuple(shift(part, axis, order, -1) for part in behind)
            groups.append(([-step, step], [*ahead, *behind]))
        else:
            last = (shift(ahead[0], axis, order, 1), shift(behind[1], axis, order, -1))
            groups.append(([-step], [*last]))
    return groups


def head_scatter(pieces, axis):
    size, mine = lax.axis_size(axis), lax.axis_index(axis)
    stride = 1
    while stride < size:
        bit = (mine // stride) % 2
        left = pieces.shape[0] // 2
        view = pieces.reshape(left, 2, *pieces.shape[1:])
        send = lax.dynamic_index_in_dim(view, 1 - bit, 1, keepdims=False)
        keep = lax.dynamic_index_in_dim(view, bit, 1, keepdims=False)
        came = lax.ppermute(send, axis, [(i, i ^ stride) for i in range(size)])
        pieces = (keep.astype(jnp.float32) + came.astype(jnp.float32)).astype(jnp.bfloat16)
        stride *= 2
    return pieces[0]


def across(x, mask):
    axes = ("seq", "head")
    return lax.ppermute(x, axes, [(i, i ^ mask) for i in range(lax.axis_size(axes))])


def hop(x, stride, edges):
    axes = ("seq", "head")
    place = [i // stride % 4 for i in range(lax.axis_size(axes))]
    pairs = [
        (i, i + (to - place[i]) * stride)
        for i in range(len(place))
        for at, to in edges
        if at == place[i]
    ]
    return lax.ppermute(x, axes, pairs)


def expert_half(slot_rows, up_weight, down_weight):
    model_width = slot_rows.shape[-1]
    flat_rows = slot_rows.reshape(-1, model_width)
    activation = jnp.dot(flat_rows, up_weight[0], preferred_element_type=jnp.float32)
    activation = jnp.maximum(activation, 0.0)
    activation = (activation * activation).astype(jnp.bfloat16)
    output = jnp.dot(activation, down_weight[0], preferred_element_type=jnp.float32).astype(
        jnp.bfloat16
    )
    return output.reshape(slot_rows.shape)


def per_device(
    ssm_values,
    ssm_gate,
    write_proj,
    read_proj,
    step_size,
    decay_power,
    skip_gain,
    norm_gain,
    out_weight,
    residual,
    expert_norm,
    router_weight,
    expert_index,
    up_weight,
    down_weight,
):
    tokens_dev = ssm_values.shape[0]
    heads_dev = step_size.shape[1]
    per_group = HEADS // GROUPS
    groups_dev = heads_dev // per_group
    count_blocks = tokens_dev // BLOCK_LEN
    weight_groups = ring_weights(out_weight, "seq")
    decay_rates = jnp.exp2(-decay_power.astype(jnp.float32))
    values = ssm_values.reshape(count_blocks, BLOCK_LEN, heads_dev, HEAD_DIM)
    steps_all = step_size.reshape(count_blocks, BLOCK_LEN, heads_dev)
    writes = write_proj.reshape(count_blocks, BLOCK_LEN, groups_dev, STATE)
    reads = read_proj.reshape(count_blocks, BLOCK_LEN, groups_dev, STATE)
    causal = jnp.tril(jnp.ones((BLOCK_LEN, BLOCK_LEN), dtype=bool))

    def one_block(pieces):
        values_in, steps_in, write_in, read_in = pieces
        log_decay = -steps_in * decay_rates[None, :]
        cumulative = jnp.cumsum(log_decay, axis=0)
        scores = jnp.einsum("tgn,sgn->gts", read_in, write_in, preferred_element_type=jnp.float32)
        scores = jnp.repeat(scores, per_group, axis=0)
        decays = jnp.exp(cumulative.T[:, :, None] - cumulative.T[:, None, :])
        mixing = jnp.where(causal[None], scores * decays * steps_in.T[:, None, :], 0.0).astype(
            jnp.bfloat16
        )
        inner_out = jnp.einsum(
            "hts,shp->thp", mixing, values_in, preferred_element_type=jnp.float32
        )
        block_total = cumulative[-1]
        weighted = (
            values_in.astype(jnp.float32)
            * (jnp.exp(block_total[None, :] - cumulative) * steps_in)[:, :, None]
        ).astype(jnp.bfloat16)
        write_heads = jnp.repeat(write_in, per_group, axis=1)
        fresh_state = jnp.einsum(
            "shp,shn->hpn", weighted, write_heads, preferred_element_type=jnp.float32
        )
        return (inner_out, fresh_state, block_total, cumulative)

    inner_all, fresh_all, totals_blk, cumul_all = lax.map(
        one_block, (values, steps_all, writes, reads)
    )

    def summarize(carried_in, pieces):
        decay_prod, summary = carried_in
        block_total, fresh_state = pieces
        factor = jnp.exp(block_total)
        return ((decay_prod * factor, factor[:, None, None] * summary + fresh_state), None)

    zero_state = jnp.zeros((heads_dev, HEAD_DIM, STATE), jnp.float32)
    (device_decay, device_state), unused = lax.scan(
        summarize, (jnp.ones((heads_dev,), jnp.float32), zero_state), (totals_blk, fresh_all)
    )

    incoming = entering(device_decay, device_state, "seq")

    def emit_rows(carry_state, pieces):
        read_in, cumulative, block_total, fresh_state = pieces
        read_heads = jnp.repeat(read_in, per_group, axis=1)
        carried = jnp.einsum(
            "thn,hpn->thp",
            read_heads,
            carry_state.astype(jnp.bfloat16),
            preferred_element_type=jnp.float32,
        )
        carried = carried * jnp.exp(cumulative)[:, :, None]
        return (jnp.exp(block_total)[:, None, None] * carry_state + fresh_state, carried)

    final_state, carried_all = lax.scan(
        emit_rows, incoming, (reads, cumul_all, totals_blk, fresh_all)
    )
    values_flat = ssm_values.reshape(tokens_dev, heads_dev, HEAD_DIM).astype(jnp.float32)
    ssm_out = (inner_all + carried_all).reshape(tokens_dev, heads_dev, HEAD_DIM) + skip_gain[
        None, :, None
    ] * values_flat
    gate_vals = ssm_gate.reshape(tokens_dev, heads_dev, HEAD_DIM).astype(jnp.float32)
    gated = (ssm_out * jax.nn.silu(gate_vals)).reshape(tokens_dev, groups_dev, per_group * HEAD_DIM)
    inv_rms = lax.rsqrt(jnp.mean(gated * gated, axis=-1, keepdims=True) + EPSILON)
    normed = (
        (gated * inv_rms).reshape(tokens_dev, heads_dev * HEAD_DIM) * norm_gain[None, :]
    ).astype(jnp.bfloat16)
    seq_size = lax.axis_size("seq")
    head_size = lax.axis_size("head")
    rows_own = tokens_dev // head_size
    shard_width = out_weight.shape[1]
    offsets, products = [], []
    for steps, parts in weight_groups:
        rows = parts[0] if len(parts) == 1 else jnp.concatenate(parts, axis=0)
        product = lax.dot_general(
            normed, rows, (((1,), (1,)), ((), ())), preferred_element_type=jnp.float32
        ).astype(jnp.bfloat16)
        for at, step in enumerate(steps):
            offsets.append(step)
            products.append(product[:, at * shard_width : (at + 1) * shard_width])
    stacked = jnp.stack(products, axis=0).reshape(
        seq_size, head_size, rows_own, shard_width
    )
    scattered = head_scatter(stacked.transpose(1, 0, 2, 3), "head").astype(jnp.float32)
    order = seq_ring(seq_size)
    table = [[0] * seq_size for _ in range(seq_size)]
    for place, index in enumerate(order):
        for at, step in enumerate(offsets):
            table[index][order[(place + step) % seq_size]] = at
    places = jnp.asarray(table, jnp.int32)[lax.axis_index("seq")]
    mixed_out = jnp.concatenate(
        [pick(scattered, places[b]) for b in range(seq_size)], axis=1
    )
    hidden = residual.astype(jnp.float32) + mixed_out
    inputs = (
        hidden
        * lax.rsqrt(jnp.mean(hidden * hidden, axis=-1, keepdims=True) + EPSILON)
        * expert_norm[None, :]
    ).astype(jnp.bfloat16)
    logits = jnp.dot(inputs, router_weight, preferred_element_type=jnp.float32)
    experts = router_weight.shape[1]
    model_width = inputs.shape[1]
    expert_hits = expert_index[:, :, None] == jnp.arange(experts, dtype=jnp.int32)[None, None, :]
    picked = jnp.sum(jnp.where(expert_hits, logits[:, None, :], 0.0), axis=-1)
    probability = jax.nn.sigmoid(picked)
    shares = ROUTE_SCALE * probability / jnp.sum(probability, axis=1, keepdims=True)
    flat_hits = expert_hits.astype(jnp.int32).reshape(rows_own * TOP, experts)
    before = jnp.cumsum(flat_hits, axis=0) - flat_hits
    slot_index = jnp.sum(before * flat_hits, axis=1).reshape(rows_own, TOP)
    capacity = 8 * TOP * tokens_dev // (3 * seq_size * head_size * head_size)
    notes = jnp.concatenate(
        [expert_index.astype(jnp.bfloat16), slot_index.astype(jnp.bfloat16), shares.astype(jnp.bfloat16)],
        axis=1,
    )
    notes = jnp.pad(notes, ((0, 0), (0, 128 - notes.shape[1])))
    moe_out = routed(
        jnp.concatenate([inputs, notes], axis=1), model_width, capacity, experts, up_weight, down_weight
    )
    return (hidden + moe_out).astype(jnp.bfloat16)


def routed(block, width, capacity, experts, up_weight, down_weight):
    inner = experts // 4
    stride = 2 * inner
    place = lax.axis_index("seq") * lax.axis_size("head") + lax.axis_index("head")
    mine_outer, mine_inner = place // stride, place // 2 % inner
    inside = (mine_outer == 1) | (mine_outer == 2)
    turned = mine_inner ^ jnp.arange(inner, dtype=jnp.int32)
    wanted = (mine_outer * inner + turned)[:, None] * capacity + jnp.arange(capacity, dtype=jnp.int32)
    wanted = wanted.reshape(-1).astype(jnp.float32)

    def placed(rows):
        notes = rows[:, width : width + 3 * TOP].astype(jnp.float32)
        code = notes[:, :TOP] * capacity + notes[:, TOP : 2 * TOP]
        match = code[:, :, None] == wanted[None, None, :]
        placing = jnp.any(match, axis=1).astype(jnp.bfloat16)
        weights = jnp.sum(jnp.where(match, notes[:, 2 * TOP :, None], 0.0), axis=1)
        return placing, weights.astype(jnp.bfloat16)

    def spread(rows):
        placing, weights = placed(rows)
        inputs = rows[:, :width]
        parts = []
        for m in range(inner):
            part = lax.dot_general(
                placing[:, m * capacity : (m + 1) * capacity],
                inputs,
                (((0,), (0,)), ((), ())),
                preferred_element_type=jnp.float32,
            ).astype(jnp.bfloat16)
            parts.append(across(part, 2 * m) if m else part)
        return parts, weights

    def expert(parts):
        own_rows = jnp.concatenate(parts, axis=0)
        other_rows = across(own_rows, 1)
        both = expert_half(jnp.concatenate([own_rows, other_rows], axis=0), up_weight, down_weight)
        half = own_rows.shape[0]
        back = across(both[half:], 1)
        return (both[:half].astype(jnp.float32) + back.astype(jnp.float32)).astype(jnp.bfloat16)

    def brought(summed):
        results = []
        for m in range(inner):
            part = summed[m * capacity : (m + 1) * capacity]
            results.append(across(part, 2 * m) if m else part)
        return results

    def home(results, weights, k):
        partial = jnp.dot(
            weights, jnp.concatenate(results, axis=0), preferred_element_type=jnp.float32
        )
        return across(partial.astype(jnp.bfloat16), k * stride) if k else partial

    near = across(block, stride)
    middle = hop(block, stride, [(1, 2), (2, 1)])
    sent0 = spread(block)
    near, middle, sent0 = lax.optimization_barrier((near, middle, sent0))

    middle_next = hop(near, stride, [(1, 2), (2, 1)])
    end_next = hop(middle, stride, [(1, 0), (2, 3)])
    sent1 = spread(near)
    done0 = expert(sent0[0])
    middle, middle_next, end_next, sent1, done0 = lax.optimization_barrier(
        (middle, middle_next, end_next, sent1, done0)
    )

    end_last = hop(middle_next, stride, [(1, 0), (2, 3)])
    sent2 = spread(jnp.where(inside, middle_next, end_next))
    done1 = expert(sent1[0])
    back0 = brought(done0)
    middle, end_last, sent2, done1, back0 = lax.optimization_barrier(
        (middle, end_last, sent2, done1, back0)
    )

    sent3 = spread(jnp.where(inside, middle, end_last))
    done2 = expert(sent2[0])
    back1 = brought(done1)
    sum0 = home(back0, sent0[1], 0)
    sent3, done2, back1, sum0 = lax.optimization_barrier((sent3, done2, back1, sum0))

    done3 = expert(sent3[0])
    back2 = brought(done2)
    sum1 = home(back1, sent1[1], 1)
    done3, back2, sum1 = lax.optimization_barrier((done3, back2, sum1))

    back3 = brought(done3)
    sum2 = home(back2, sent2[1], 2)
    back3, sum2 = lax.optimization_barrier((back3, sum2))

    sum3 = home(back3, sent3[1], 3)
    total = sum0
    for part in (sum1, sum2, sum3):
        total = total + part.astype(jnp.float32)
    return total


def solution(mesh):
    return jax.shard_map(
        per_device,
        mesh=mesh,
        in_specs=(
            P(("grp", "seq"), "head"),
            P(("grp", "seq"), "head"),
            P(("grp", "seq"), "head"),
            P(("grp", "seq"), "head"),
            P(("grp", "seq"), "head"),
            P("head"),
            P("head"),
            P("head"),
            P("head", "seq"),
            P(("grp", "seq", "head"), None),
            P(),
            P(),
            P(("grp", "seq", "head"), None),
            P(("seq", "head"), None, None),
            P(("seq", "head"), None, None),
        ),
        out_specs=P(("grp", "seq", "head"), None),
        check_vma=False,
    )
```

```python
import jax
import jax.numpy as jnp
from jax import lax
from jax.sharding import PartitionSpec as P


HEADS = 64
HEAD_DIM = 64
STATE = 128
GROUPS = 8
TOP = 6
BLOCK_LEN = 256


EPSILON = 1e-05
ROUTE_SCALE = 2.5


def seq_ring(size):
    return list(range(0, size, 2)) + list(range(1, size, 2))[::-1]


def shift(x, axis, order, step):
    size = len(order)
    return lax.ppermute(x, axis, [(order[i], order[(i + step) % size]) for i in range(size)])


def pick(parts, index):
    return lax.dynamic_index_in_dim(parts, index, 0, keepdims=False)


def packed(state, decay):
    high = decay.astype(jnp.bfloat16)
    low = (decay - high.astype(jnp.float32)).astype(jnp.bfloat16)
    rows = jnp.zeros((16, STATE), jnp.bfloat16)
    rows = rows.at[0, : decay.shape[0]].set(high).at[1, : decay.shape[0]].set(low)
    return jnp.concatenate([state.reshape(-1, STATE).astype(jnp.bfloat16), rows], axis=0)


def unpacked(block, heads):
    rows = heads * HEAD_DIM
    state = block[:rows].astype(jnp.float32).reshape(heads, HEAD_DIM, STATE)
    decay = block[rows, :heads].astype(jnp.float32) + block[rows + 1, :heads].astype(jnp.float32)
    return state, decay


def swapped(decay, state, axis):
    size, side = lax.axis_size(axis), lax.axis_index(axis) % 2
    half = decay.shape[0] // 2
    states = state.reshape(2, half, HEAD_DIM, STATE)
    decays = decay.reshape(2, half)
    return lax.ppermute(
        packed(pick(states, 1 - side), pick(decays, 1 - side)),
        axis,
        [(i, i ^ 1) for i in range(size)],
    )


def entering(got, decay, state, axis):
    size, side = lax.axis_size(axis), lax.axis_index(axis) % 2
    odd = side == 1
    half = decay.shape[0] // 2
    other_state, other_decay = unpacked(got, half)
    own_state = pick(state.reshape(2, half, HEAD_DIM, STATE), side)
    own_decay = pick(decay.reshape(2, half), side)
    first_state = jnp.where(odd, other_state, own_state)
    second_state = jnp.where(odd, own_state, other_state)
    first_decay = jnp.where(odd, other_decay, own_decay)
    second_decay = jnp.where(odd, own_decay, other_decay)
    pair = packed(
        second_decay[:, None, None] * first_state + second_state, first_decay * second_decay
    )
    before = jnp.zeros_like(first_state)
    received = [
        lax.ppermute(pair, axis, [(i, i + 2 * d) for i in range(size - 2 * d)])
        for d in range(1, size // 2)
    ]
    for block in received[::-1]:
        block_state, block_decay = unpacked(block, half)
        before = block_decay[:, None, None] * before + block_state
    inner = first_decay[:, None, None] * before + first_state
    mine_half = jnp.where(odd, inner, before)
    send_half = jnp.where(odd, before, inner).astype(jnp.bfloat16)
    back = lax.ppermute(
        send_half.reshape(-1, STATE), axis, [(i, i ^ 1) for i in range(size)]
    )
    back = back.astype(jnp.float32).reshape(mine_half.shape)
    low = jnp.where(odd, back, mine_half)
    high = jnp.where(odd, mine_half, back)
    return jnp.concatenate([low, high], axis=0)


def ring_step(parts, axis, step):
    size = lax.axis_size(axis)
    order = seq_ring(size)
    ahead, behind = parts
    if 2 * step < size:
        ahead = tuple(shift(part, axis, order, 1) for part in ahead)
        behind = tuple(shift(part, axis, order, -1) for part in behind)
        return ahead, behind
    return (shift(ahead[0], axis, order, 1),), (shift(behind[1], axis, order, -1),)


def head_scatter(pieces, axis):
    size, mine = lax.axis_size(axis), lax.axis_index(axis)
    stride = 1
    while stride < size:
        bit = (mine // stride) % 2
        left = pieces.shape[0] // 2
        view = pieces.reshape(left, 2, *pieces.shape[1:])
        send = lax.dynamic_index_in_dim(view, 1 - bit, 1, keepdims=False)
        keep = lax.dynamic_index_in_dim(view, bit, 1, keepdims=False)
        came = lax.ppermute(send, axis, [(i, i ^ stride) for i in range(size)])
        pieces = (keep.astype(jnp.float32) + came.astype(jnp.float32)).astype(jnp.bfloat16)
        stride *= 2
    return pieces[0]


def across(x, mask):
    axes = ("seq", "head")
    return lax.ppermute(x, axes, [(i, i ^ mask) for i in range(lax.axis_size(axes))])


def expert_half(slot_rows, up_weight, down_weight):
    model_width = slot_rows.shape[-1]
    flat_rows = slot_rows.reshape(-1, model_width)
    activation = jnp.dot(flat_rows, up_weight[0], preferred_element_type=jnp.float32)
    activation = jnp.maximum(activation, 0.0)
    activation = (activation * activation).astype(jnp.bfloat16)
    output = jnp.dot(activation, down_weight[0], preferred_element_type=jnp.float32).astype(
        jnp.bfloat16
    )
    return output.reshape(slot_rows.shape)


def per_device(
    ssm_values,
    ssm_gate,
    write_proj,
    read_proj,
    step_size,
    decay_power,
    skip_gain,
    norm_gain,
    out_weight,
    residual,
    expert_norm,
    router_weight,
    expert_index,
    up_weight,
    down_weight,
):
    tokens_dev = ssm_values.shape[0]
    heads_dev = step_size.shape[1]
    per_group = HEADS // GROUPS
    groups_dev = heads_dev // per_group
    count_blocks = tokens_dev // BLOCK_LEN
    seq_size = lax.axis_size("seq")
    head_size = lax.axis_size("head")
    shard = out_weight.T
    cut = (shard.shape[0] // 2 + 15) // 16 * 16
    halves = (shard[:cut], shard[cut:])
    ring = [ring_step((halves, halves), "seq", 1)]
    decay_rates = jnp.exp2(-decay_power.astype(jnp.float32))
    values = ssm_values.reshape(count_blocks, BLOCK_LEN, heads_dev, HEAD_DIM)
    steps_all = step_size.reshape(count_blocks, BLOCK_LEN, heads_dev)
    writes = write_proj.reshape(count_blocks, BLOCK_LEN, groups_dev, STATE)
    reads = read_proj.reshape(count_blocks, BLOCK_LEN, groups_dev, STATE)
    causal = jnp.tril(jnp.ones((BLOCK_LEN, BLOCK_LEN), dtype=bool))

    def one_block(pieces):
        values_in, steps_in, write_in, read_in = pieces
        log_decay = -steps_in * decay_rates[None, :]
        cumulative = jnp.cumsum(log_decay, axis=0)
        scores = jnp.einsum("tgn,sgn->gts", read_in, write_in, preferred_element_type=jnp.float32)
        scores = jnp.repeat(scores, per_group, axis=0)
        decays = jnp.exp(cumulative.T[:, :, None] - cumulative.T[:, None, :])
        mixing = jnp.where(causal[None], scores * decays * steps_in.T[:, None, :], 0.0).astype(
            jnp.bfloat16
        )
        inner_out = jnp.einsum(
            "hts,shp->thp", mixing, values_in, preferred_element_type=jnp.float32
        )
        block_total = cumulative[-1]
        weighted = (
            values_in.astype(jnp.float32)
            * (jnp.exp(block_total[None, :] - cumulative) * steps_in)[:, :, None]
        ).astype(jnp.bfloat16)
        write_heads = jnp.repeat(write_in, per_group, axis=1)
        fresh_state = jnp.einsum(
            "shp,shn->hpn", weighted, write_heads, preferred_element_type=jnp.float32
        )
        return (inner_out, fresh_state, block_total, cumulative)

    inner_all, fresh_all, totals_blk, cumul_all = lax.map(
        one_block, (values, steps_all, writes, reads)
    )

    def summarize(carried_in, pieces):
        decay_prod, summary = carried_in
        block_total, fresh_state = pieces
        factor = jnp.exp(block_total)
        return ((decay_prod * factor, factor[:, None, None] * summary + fresh_state), None)

    zero_state = jnp.zeros((heads_dev, HEAD_DIM, STATE), jnp.float32)
    (device_decay, device_state), unused = lax.scan(
        summarize, (jnp.ones((heads_dev,), jnp.float32), zero_state), (totals_blk, fresh_all)
    )

    got = swapped(device_decay, device_state, "seq")
    ring[0], got = lax.optimization_barrier((ring[0], got))
    for step in range(2, seq_size // 2 + 1):
        ring.append(ring_step(ring[-1], "seq", step))
    incoming = entering(got, device_decay, device_state, "seq")

    def emit_rows(carry_state, pieces):
        read_in, cumulative, block_total, fresh_state = pieces
        read_heads = jnp.repeat(read_in, per_group, axis=1)
        carried = jnp.einsum(
            "thn,hpn->thp",
            read_heads,
            carry_state.astype(jnp.bfloat16),
            preferred_element_type=jnp.float32,
        )
        carried = carried * jnp.exp(cumulative)[:, :, None]
        return (jnp.exp(block_total)[:, None, None] * carry_state + fresh_state, carried)

    _, carried_all = lax.scan(emit_rows, incoming, (reads, cumul_all, totals_blk, fresh_all))
    values_flat = ssm_values.reshape(tokens_dev, heads_dev, HEAD_DIM).astype(jnp.float32)
    ssm_out = (inner_all + carried_all).reshape(tokens_dev, heads_dev, HEAD_DIM) + skip_gain[
        None, :, None
    ] * values_flat
    gate_vals = ssm_gate.reshape(tokens_dev, heads_dev, HEAD_DIM).astype(jnp.float32)
    gated = (ssm_out * jax.nn.silu(gate_vals)).reshape(tokens_dev, groups_dev, per_group * HEAD_DIM)
    inv_rms = lax.rsqrt(jnp.mean(gated * gated, axis=-1, keepdims=True) + EPSILON)
    normed = (
        (gated * inv_rms).reshape(tokens_dev, heads_dev * HEAD_DIM) * norm_gain[None, :]
    ).astype(jnp.bfloat16)
    rows_own = tokens_dev // head_size
    shard_width = out_weight.shape[1]

    def product(parts):
        rows = parts[0] if len(parts) == 1 else jnp.concatenate(parts, axis=0)
        result = lax.dot_general(
            normed, rows, (((1,), (1,)), ((), ())), preferred_element_type=jnp.float32
        ).astype(jnp.bfloat16)
        return [
            result[:, at : at + shard_width].reshape(head_size, 1, rows_own, shard_width)
            for at in range(0, result.shape[1], shard_width)
        ]

    offsets, products = [0], product([shard])
    batches = []
    for step in range(1, seq_size // 2 + 1):
        ahead, behind = ring[step - 1]
        offsets += [-step, step] if 2 * step < seq_size else [-step]
        products += product([*ahead, *behind])
        if step in (seq_size // 4, seq_size // 2):
            batches.append(head_scatter(jnp.concatenate(products, axis=1), "head"))
            products = []
    scattered = jnp.concatenate(batches, axis=0).astype(jnp.float32)
    order = seq_ring(seq_size)
    table = [[0] * seq_size for _ in range(seq_size)]
    for place, index in enumerate(order):
        for at, step in enumerate(offsets):
            table[index][order[(place + step) % seq_size]] = at
    places = jnp.asarray(table, jnp.int32)[lax.axis_index("seq")]
    mixed_out = jnp.concatenate(
        [pick(scattered, places[b]) for b in range(seq_size)], axis=1
    )
    hidden = residual.astype(jnp.float32) + mixed_out
    inputs = (
        hidden
        * lax.rsqrt(jnp.mean(hidden * hidden, axis=-1, keepdims=True) + EPSILON)
        * expert_norm[None, :]
    ).astype(jnp.bfloat16)
    logits = jnp.dot(inputs, router_weight, preferred_element_type=jnp.float32)
    experts = router_weight.shape[1]
    model_width = inputs.shape[1]
    expert_hits = expert_index[:, :, None] == jnp.arange(experts, dtype=jnp.int32)[None, None, :]
    picked = jnp.sum(jnp.where(expert_hits, logits[:, None, :], 0.0), axis=-1)
    probability = jax.nn.sigmoid(picked)
    shares = ROUTE_SCALE * probability / jnp.sum(probability, axis=1, keepdims=True)
    flat_hits = expert_hits.astype(jnp.int32).reshape(rows_own * TOP, experts)
    before = jnp.cumsum(flat_hits, axis=0) - flat_hits
    slot_index = jnp.sum(before * flat_hits, axis=1).reshape(rows_own, TOP)
    capacity = 8 * TOP * tokens_dev // (3 * seq_size * head_size * head_size)
    notes = jnp.concatenate(
        [expert_index.astype(jnp.bfloat16), slot_index.astype(jnp.bfloat16), shares.astype(jnp.bfloat16)],
        axis=1,
    )
    notes = jnp.pad(notes, ((0, 0), (0, 128 - notes.shape[1])))
    moe_out = routed(
        jnp.concatenate([inputs, notes], axis=1), model_width, capacity, experts, up_weight, down_weight
    )
    return (hidden + moe_out).astype(jnp.bfloat16)


def routed(block, width, capacity, experts, up_weight, down_weight):
    inner = experts // 4
    stride = 2 * inner
    place = lax.axis_index("seq") * lax.axis_size("head") + lax.axis_index("head")
    mine_outer, mine_inner = place // stride, place // 2 % inner
    turned = mine_inner ^ jnp.arange(inner, dtype=jnp.int32)
    wanted = (mine_outer * inner + turned)[:, None] * capacity + jnp.arange(capacity, dtype=jnp.int32)
    wanted = wanted.reshape(-1).astype(jnp.float32)

    def placed(rows):
        notes = rows[:, width : width + 3 * TOP].astype(jnp.float32)
        code = notes[:, :TOP] * capacity + notes[:, TOP : 2 * TOP]
        match = code[:, :, None] == wanted[None, None, :]
        placing = jnp.any(match, axis=1).astype(jnp.bfloat16)
        weights = jnp.sum(jnp.where(match, notes[:, 2 * TOP :, None], 0.0), axis=1)
        return placing, weights.astype(jnp.bfloat16)

    def spread(rows):
        placing, weights = placed(rows)
        inputs = rows[:, :width]
        parts = []
        for m in range(inner):
            part = lax.dot_general(
                placing[:, m * capacity : (m + 1) * capacity],
                inputs,
                (((0,), (0,)), ((), ())),
                preferred_element_type=jnp.float32,
            ).astype(jnp.bfloat16)
            parts.append(across(part, 2 * m) if m else part)
        return parts, weights

    def expert(parts):
        own_rows = jnp.concatenate(parts, axis=0)
        other_rows = across(own_rows, 1)
        rows = jnp.concatenate([own_rows, other_rows], axis=0)
        both = expert_half(rows, up_weight, down_weight)
        half = own_rows.shape[0]
        back = across(both[half:], 1)
        return (both[:half].astype(jnp.float32) + back.astype(jnp.float32)).astype(jnp.bfloat16)

    def brought(summed):
        results = []
        for m in range(inner):
            part = summed[m * capacity : (m + 1) * capacity]
            results.append(across(part, 2 * m) if m else part)
        return results

    def home(results, weights, k):
        partial = jnp.dot(
            weights, jnp.concatenate(results, axis=0), preferred_element_type=jnp.float32
        )
        return across(partial.astype(jnp.bfloat16), k * stride) if k else partial

    def line(k):
        return across(block, k * stride)

    rows1 = line(1)
    sent0 = spread(block)
    rows1, sent0, block = lax.optimization_barrier((rows1, sent0, block))

    rows2 = line(2)
    sent1 = spread(rows1)
    done0 = expert(sent0[0])
    rows2, sent1, done0, block = lax.optimization_barrier((rows2, sent1, done0, block))

    rows3 = line(3)
    sent2 = spread(rows2)
    done1 = expert(sent1[0])
    back0 = brought(done0)
    rows3, sent2, done1, back0 = lax.optimization_barrier((rows3, sent2, done1, back0))

    sent3 = spread(rows3)
    done2 = expert(sent2[0])
    back1 = brought(done1)
    sum0 = home(back0, sent0[1], 0)
    sent3, done2, back1, sum0 = lax.optimization_barrier((sent3, done2, back1, sum0))

    done3 = expert(sent3[0])
    back2 = brought(done2)
    sum1 = home(back1, sent1[1], 1)
    back3 = brought(done3)
    sum2 = home(back2, sent2[1], 2)
    sum3 = home(back3, sent3[1], 3)
    total = sum0
    for part in (sum1, sum2, sum3):
        total = total + part.astype(jnp.float32)
    return total


def solution(mesh):
    return jax.shard_map(
        per_device,
        mesh=mesh,
        in_specs=(
            P(("grp", "seq"), "head"),
            P(("grp", "seq"), "head"),
            P(("grp", "seq"), "head"),
            P(("grp", "seq"), "head"),
            P(("grp", "seq"), "head"),
            P("head"),
            P("head"),
            P("head"),
            P("head", "seq"),
            P(("grp", "seq", "head"), None),
            P(),
            P(),
            P(("grp", "seq", "head"), None),
            P(("seq", "head"), None, None),
            P(("seq", "head"), None, None),
        ),
        out_specs=P(("grp", "seq", "head"), None),
        check_vma=False,
    )
```

```python
import jax
import jax.numpy as jnp
from jax import lax
from jax.sharding import PartitionSpec as P


HEADS = 64
HEAD_DIM = 64
STATE = 128
GROUPS = 8
TOP = 6
BLOCK_LEN = 256


EPSILON = 1e-05
ROUTE_SCALE = 2.5


def seq_ring(size):
    return list(range(0, size, 2)) + list(range(1, size, 2))[::-1]


def shift(x, axis, order, step):
    size = len(order)
    return lax.ppermute(x, axis, [(order[i], order[(i + step) % size]) for i in range(size)])


def pick(parts, index):
    return lax.dynamic_index_in_dim(parts, index, 0, keepdims=False)


def packed(state, decay):
    high = decay.astype(jnp.bfloat16)
    low = (decay - high.astype(jnp.float32)).astype(jnp.bfloat16)
    rows = jnp.zeros((16, STATE), jnp.bfloat16)
    rows = rows.at[0, : decay.shape[0]].set(high).at[1, : decay.shape[0]].set(low)
    return jnp.concatenate([state.reshape(-1, STATE).astype(jnp.bfloat16), rows], axis=0)


def unpacked(block, heads):
    rows = heads * HEAD_DIM
    state = block[:rows].astype(jnp.float32).reshape(heads, HEAD_DIM, STATE)
    decay = block[rows, :heads].astype(jnp.float32) + block[rows + 1, :heads].astype(jnp.float32)
    return state, decay


def swapped(decay, state, axis):
    size, side = lax.axis_size(axis), lax.axis_index(axis) % 2
    half = decay.shape[0] // 2
    states = state.reshape(2, half, HEAD_DIM, STATE)
    decays = decay.reshape(2, half)
    return lax.ppermute(
        packed(pick(states, 1 - side), pick(decays, 1 - side)),
        axis,
        [(i, i ^ 1) for i in range(size)],
    )


def entering(got, decay, state, axis):
    size, side = lax.axis_size(axis), lax.axis_index(axis) % 2
    odd = side == 1
    half = decay.shape[0] // 2
    other_state, other_decay = unpacked(got, half)
    own_state = pick(state.reshape(2, half, HEAD_DIM, STATE), side)
    own_decay = pick(decay.reshape(2, half), side)
    first_state = jnp.where(odd, other_state, own_state)
    second_state = jnp.where(odd, own_state, other_state)
    first_decay = jnp.where(odd, other_decay, own_decay)
    second_decay = jnp.where(odd, own_decay, other_decay)
    pair = packed(
        second_decay[:, None, None] * first_state + second_state, first_decay * second_decay
    )
    before = jnp.zeros_like(first_state)
    received = [
        lax.ppermute(pair, axis, [(i, i + 2 * d) for i in range(size - 2 * d)])
        for d in range(1, size // 2)
    ]
    for block in received[::-1]:
        block_state, block_decay = unpacked(block, half)
        before = block_decay[:, None, None] * before + block_state
    inner = first_decay[:, None, None] * before + first_state
    mine_half = jnp.where(odd, inner, before)
    send_half = jnp.where(odd, before, inner).astype(jnp.bfloat16)
    back = lax.ppermute(
        send_half.reshape(-1, STATE), axis, [(i, i ^ 1) for i in range(size)]
    )
    back = back.astype(jnp.float32).reshape(mine_half.shape)
    low = jnp.where(odd, back, mine_half)
    high = jnp.where(odd, mine_half, back)
    return jnp.concatenate([low, high], axis=0)


def ring_step(parts, axis, step):
    size = lax.axis_size(axis)
    order = seq_ring(size)
    ahead, behind = parts
    if 2 * step < size:
        ahead = tuple(shift(part, axis, order, 1) for part in ahead)
        behind = tuple(shift(part, axis, order, -1) for part in behind)
        return ahead, behind
    return (shift(ahead[0], axis, order, 1),), (shift(behind[1], axis, order, -1),)


def head_scatter(pieces, axis):
    size, mine = lax.axis_size(axis), lax.axis_index(axis)
    stride = 1
    while stride < size:
        bit = (mine // stride) % 2
        left = pieces.shape[0] // 2
        view = pieces.reshape(left, 2, *pieces.shape[1:])
        send = lax.dynamic_index_in_dim(view, 1 - bit, 1, keepdims=False)
        keep = lax.dynamic_index_in_dim(view, bit, 1, keepdims=False)
        came = lax.ppermute(send, axis, [(i, i ^ stride) for i in range(size)])
        pieces = (keep.astype(jnp.float32) + came.astype(jnp.float32)).astype(jnp.bfloat16)
        stride *= 2
    return pieces[0]


def across(x, mask):
    axes = ("seq", "head")
    return lax.ppermute(x, axes, [(i, i ^ mask) for i in range(lax.axis_size(axes))])


def expert_half(slot_rows, up_weight, down_weight):
    model_width = slot_rows.shape[-1]
    flat_rows = slot_rows.reshape(-1, model_width)
    activation = jnp.dot(flat_rows, up_weight[0], preferred_element_type=jnp.float32)
    activation = jnp.maximum(activation, 0.0)
    activation = (activation * activation).astype(jnp.bfloat16)
    output = jnp.dot(activation, down_weight[0], preferred_element_type=jnp.float32).astype(
        jnp.bfloat16
    )
    return output.reshape(slot_rows.shape)


def per_device(
    ssm_values,
    ssm_gate,
    write_proj,
    read_proj,
    step_size,
    decay_power,
    skip_gain,
    norm_gain,
    out_weight,
    residual,
    expert_norm,
    router_weight,
    expert_index,
    up_weight,
    down_weight,
):
    tokens_dev = ssm_values.shape[0]
    heads_dev = step_size.shape[1]
    per_group = HEADS // GROUPS
    groups_dev = heads_dev // per_group
    count_blocks = tokens_dev // BLOCK_LEN
    seq_size = lax.axis_size("seq")
    head_size = lax.axis_size("head")
    shard = out_weight.T
    cut = (shard.shape[0] // 2 + 15) // 16 * 16
    halves = (shard[:cut], shard[cut:])
    ring = [ring_step((halves, halves), "seq", 1)]
    decay_rates = jnp.exp2(-decay_power.astype(jnp.float32))
    values = ssm_values.reshape(count_blocks, BLOCK_LEN, heads_dev, HEAD_DIM)
    steps_all = step_size.reshape(count_blocks, BLOCK_LEN, heads_dev)
    writes = write_proj.reshape(count_blocks, BLOCK_LEN, groups_dev, STATE)
    reads = read_proj.reshape(count_blocks, BLOCK_LEN, groups_dev, STATE)
    causal = jnp.tril(jnp.ones((BLOCK_LEN, BLOCK_LEN), dtype=bool))

    def one_block(pieces):
        values_in, steps_in, write_in, read_in = pieces
        log_decay = -steps_in * decay_rates[None, :]
        cumulative = jnp.cumsum(log_decay, axis=0)
        scores = jnp.einsum("tgn,sgn->gts", read_in, write_in, preferred_element_type=jnp.float32)
        scores = jnp.repeat(scores, per_group, axis=0)
        decays = jnp.exp(cumulative.T[:, :, None] - cumulative.T[:, None, :])
        mixing = jnp.where(causal[None], scores * decays * steps_in.T[:, None, :], 0.0).astype(
            jnp.bfloat16
        )
        inner_out = jnp.einsum(
            "hts,shp->thp", mixing, values_in, preferred_element_type=jnp.float32
        )
        block_total = cumulative[-1]
        weighted = (
            values_in.astype(jnp.float32)
            * (jnp.exp(block_total[None, :] - cumulative) * steps_in)[:, :, None]
        ).astype(jnp.bfloat16)
        write_heads = jnp.repeat(write_in, per_group, axis=1)
        fresh_state = jnp.einsum(
            "shp,shn->hpn", weighted, write_heads, preferred_element_type=jnp.float32
        )
        return (inner_out, fresh_state, block_total, cumulative)

    inner_all, fresh_all, totals_blk, cumul_all = lax.map(
        one_block, (values, steps_all, writes, reads)
    )

    def summarize(carried_in, pieces):
        decay_prod, summary = carried_in
        block_total, fresh_state = pieces
        factor = jnp.exp(block_total)
        return ((decay_prod * factor, factor[:, None, None] * summary + fresh_state), None)

    zero_state = jnp.zeros((heads_dev, HEAD_DIM, STATE), jnp.float32)
    (device_decay, device_state), unused = lax.scan(
        summarize, (jnp.ones((heads_dev,), jnp.float32), zero_state), (totals_blk, fresh_all)
    )

    got = swapped(device_decay, device_state, "seq")
    for step in range(2, seq_size // 2 + 1):
        ring.append(ring_step(ring[-1], "seq", step))
    incoming = entering(got, device_decay, device_state, "seq")

    def emit_rows(carry_state, pieces):
        read_in, cumulative, block_total, fresh_state = pieces
        read_heads = jnp.repeat(read_in, per_group, axis=1)
        carried = jnp.einsum(
            "thn,hpn->thp",
            read_heads,
            carry_state.astype(jnp.bfloat16),
            preferred_element_type=jnp.float32,
        )
        carried = carried * jnp.exp(cumulative)[:, :, None]
        return (jnp.exp(block_total)[:, None, None] * carry_state + fresh_state, carried)

    _, carried_all = lax.scan(emit_rows, incoming, (reads, cumul_all, totals_blk, fresh_all))
    values_flat = ssm_values.reshape(tokens_dev, heads_dev, HEAD_DIM).astype(jnp.float32)
    ssm_out = (inner_all + carried_all).reshape(tokens_dev, heads_dev, HEAD_DIM) + skip_gain[
        None, :, None
    ] * values_flat
    gate_vals = ssm_gate.reshape(tokens_dev, heads_dev, HEAD_DIM).astype(jnp.float32)
    gated = (ssm_out * jax.nn.silu(gate_vals)).reshape(tokens_dev, groups_dev, per_group * HEAD_DIM)
    inv_rms = lax.rsqrt(jnp.mean(gated * gated, axis=-1, keepdims=True) + EPSILON)
    normed = (
        (gated * inv_rms).reshape(tokens_dev, heads_dev * HEAD_DIM) * norm_gain[None, :]
    ).astype(jnp.bfloat16)
    rows_own = tokens_dev // head_size
    shard_width = out_weight.shape[1]

    def product(parts):
        rows = parts[0] if len(parts) == 1 else jnp.concatenate(parts, axis=0)
        result = lax.dot_general(
            normed, rows, (((1,), (1,)), ((), ())), preferred_element_type=jnp.float32
        ).astype(jnp.bfloat16)
        return [
            result[:, at : at + shard_width].reshape(head_size, 1, rows_own, shard_width)
            for at in range(0, result.shape[1], shard_width)
        ]

    offsets, products = [0], product([shard])
    batches = []
    for step in range(1, seq_size // 2 + 1):
        ahead, behind = ring[step - 1]
        offsets += [-step, step] if 2 * step < seq_size else [-step]
        products += product([*ahead, *behind])
        if step in (seq_size // 4, seq_size // 2 - 1, seq_size // 2):
            batches.append(head_scatter(jnp.concatenate(products, axis=1), "head"))
            products = []
    scattered = jnp.concatenate(batches, axis=0).astype(jnp.float32)
    order = seq_ring(seq_size)
    table = [[0] * seq_size for _ in range(seq_size)]
    for place, index in enumerate(order):
        for at, step in enumerate(offsets):
            table[index][order[(place + step) % seq_size]] = at
    places = jnp.asarray(table, jnp.int32)[lax.axis_index("seq")]
    mixed_out = jnp.concatenate(
        [pick(scattered, places[b]) for b in range(seq_size)], axis=1
    )
    hidden = residual.astype(jnp.float32) + mixed_out
    inputs = (
        hidden
        * lax.rsqrt(jnp.mean(hidden * hidden, axis=-1, keepdims=True) + EPSILON)
        * expert_norm[None, :]
    ).astype(jnp.bfloat16)
    logits = jnp.dot(inputs, router_weight, preferred_element_type=jnp.float32)
    experts = router_weight.shape[1]
    model_width = inputs.shape[1]
    expert_hits = expert_index[:, :, None] == jnp.arange(experts, dtype=jnp.int32)[None, None, :]
    picked = jnp.sum(jnp.where(expert_hits, logits[:, None, :], 0.0), axis=-1)
    probability = jax.nn.sigmoid(picked)
    shares = ROUTE_SCALE * probability / jnp.sum(probability, axis=1, keepdims=True)
    flat_hits = expert_hits.astype(jnp.int32).reshape(rows_own * TOP, experts)
    before = jnp.cumsum(flat_hits, axis=0) - flat_hits
    slot_index = jnp.sum(before * flat_hits, axis=1).reshape(rows_own, TOP)
    capacity = 8 * TOP * tokens_dev // (3 * seq_size * head_size * head_size)
    notes = jnp.concatenate(
        [expert_index.astype(jnp.bfloat16), slot_index.astype(jnp.bfloat16), shares.astype(jnp.bfloat16)],
        axis=1,
    )
    notes = jnp.pad(notes, ((0, 0), (0, 128 - notes.shape[1])))
    moe_out = routed(
        jnp.concatenate([inputs, notes], axis=1), model_width, capacity, experts, up_weight, down_weight
    )
    return (hidden + moe_out).astype(jnp.bfloat16)


def routed(block, width, capacity, experts, up_weight, down_weight):
    inner = experts // 4
    stride = 2 * inner
    place = lax.axis_index("seq") * lax.axis_size("head") + lax.axis_index("head")
    mine_outer, mine_inner = place // stride, place // 2 % inner
    turned = mine_inner ^ jnp.arange(inner, dtype=jnp.int32)
    wanted = (mine_outer * inner + turned)[:, None] * capacity + jnp.arange(capacity, dtype=jnp.int32)
    wanted = wanted.reshape(-1).astype(jnp.float32)

    def placed(rows):
        notes = rows[:, width : width + 3 * TOP].astype(jnp.float32)
        code = notes[:, :TOP] * capacity + notes[:, TOP : 2 * TOP]
        match = code[:, :, None] == wanted[None, None, :]
        placing = jnp.any(match, axis=1).astype(jnp.bfloat16)
        weights = jnp.sum(jnp.where(match, notes[:, 2 * TOP :, None], 0.0), axis=1)
        return placing, weights.astype(jnp.bfloat16)

    def spread(rows):
        placing, weights = placed(rows)
        inputs = rows[:, :width]
        parts = []
        for m in range(inner):
            part = lax.dot_general(
                placing[:, m * capacity : (m + 1) * capacity],
                inputs,
                (((0,), (0,)), ((), ())),
                preferred_element_type=jnp.float32,
            ).astype(jnp.bfloat16)
            parts.append(across(part, 2 * m) if m else part)
        return parts, weights

    def expert(parts):
        own_rows = jnp.concatenate(parts, axis=0)
        other_rows = across(own_rows, 1)
        rows = jnp.concatenate([own_rows, other_rows], axis=0)
        both = expert_half(rows, up_weight, down_weight)
        half = own_rows.shape[0]
        back = across(both[half:], 1)
        return (both[:half].astype(jnp.float32) + back.astype(jnp.float32)).astype(jnp.bfloat16)

    def brought(summed):
        results = []
        for m in range(inner):
            part = summed[m * capacity : (m + 1) * capacity]
            results.append(across(part, 2 * m) if m else part)
        return results

    def home(results, weights, k):
        partial = jnp.dot(
            weights, jnp.concatenate(results, axis=0), preferred_element_type=jnp.float32
        )
        return across(partial.astype(jnp.bfloat16), k * stride) if k else partial

    def line(k):
        return across(block, k * stride)

    rows1, rows2 = line(1), line(2)
    sent0 = spread(block)
    rows1, sent0, block = lax.optimization_barrier((rows1, sent0, block))

    rows3 = line(3)
    sent1 = spread(rows1)
    done0 = expert(sent0[0])
    rows2, sent1, done0 = lax.optimization_barrier((rows2, sent1, done0))

    sent2 = spread(rows2)
    done1 = expert(sent1[0])
    back0 = brought(done0)
    rows3, sent2, done1, back0 = lax.optimization_barrier((rows3, sent2, done1, back0))

    sent3 = spread(rows3)
    done2 = expert(sent2[0])
    back1 = brought(done1)
    sum0 = home(back0, sent0[1], 0)
    sent3, done2, back1, sum0 = lax.optimization_barrier((sent3, done2, back1, sum0))

    done3 = expert(sent3[0])
    back2 = brought(done2)
    sum1 = home(back1, sent1[1], 1)
    back3 = brought(done3)
    sum2 = home(back2, sent2[1], 2)
    sum3 = home(back3, sent3[1], 3)
    total = sum0
    for part in (sum1, sum2, sum3):
        total = total + part.astype(jnp.float32)
    return total


def solution(mesh):
    return jax.shard_map(
        per_device,
        mesh=mesh,
        in_specs=(
            P(("grp", "seq"), "head"),
            P(("grp", "seq"), "head"),
            P(("grp", "seq"), "head"),
            P(("grp", "seq"), "head"),
            P(("grp", "seq"), "head"),
            P("head"),
            P("head"),
            P("head"),
            P("head", "seq"),
            P(("grp", "seq", "head"), None),
            P(),
            P(),
            P(("grp", "seq", "head"), None),
            P(("seq", "head"), None, None),
            P(("seq", "head"), None, None),
        ),
        out_specs=P(("grp", "seq", "head"), None),
        check_vma=False,
    )
```

```python
import jax
import jax.numpy as jnp
from jax import lax
from jax.sharding import PartitionSpec as P


HEADS = 64
HEAD_DIM = 64
STATE = 128
GROUPS = 8
TOP = 6
BLOCK_LEN = 256


EPSILON = 1e-05
ROUTE_SCALE = 2.5


def seq_ring(size):
    return list(range(0, size, 2)) + list(range(1, size, 2))[::-1]


def shift(x, axis, order, step):
    size = len(order)
    return lax.ppermute(x, axis, [(order[i], order[(i + step) % size]) for i in range(size)])


def pick(parts, index):
    return lax.dynamic_index_in_dim(
        parts, index, 0, keepdims=False, allow_negative_indices=False
    )


def packed(state, decay):
    high = decay.astype(jnp.bfloat16)
    low = (decay - high.astype(jnp.float32)).astype(jnp.bfloat16)
    rows = jnp.zeros((16, STATE), jnp.bfloat16)
    rows = rows.at[0, : decay.shape[0]].set(high).at[1, : decay.shape[0]].set(low)
    return jnp.concatenate([state.reshape(-1, STATE).astype(jnp.bfloat16), rows], axis=0)


def unpacked(block, heads):
    rows = heads * HEAD_DIM
    state = block[:rows].astype(jnp.float32).reshape(heads, HEAD_DIM, STATE)
    decay = block[rows, :heads].astype(jnp.float32) + block[rows + 1, :heads].astype(jnp.float32)
    return state, decay


def swapped(decay, state, axis):
    size, side = lax.axis_size(axis), lax.axis_index(axis) & 1
    half = decay.shape[0] // 2
    states = state.reshape(2, half, HEAD_DIM, STATE)
    decays = decay.reshape(2, half)
    return lax.ppermute(
        packed(pick(states, 1 - side), pick(decays, 1 - side)),
        axis,
        [(i, i ^ 1) for i in range(size)],
    )


def entering(got, decay, state, axis):
    size, side = lax.axis_size(axis), lax.axis_index(axis) & 1
    odd = side == 1
    half = decay.shape[0] // 2
    other_state, other_decay = unpacked(got, half)
    own_state = pick(state.reshape(2, half, HEAD_DIM, STATE), side)
    own_decay = pick(decay.reshape(2, half), side)
    first_state = jnp.where(odd, other_state, own_state)
    first_decay = jnp.where(odd, other_decay, own_decay)
    second_decay = jnp.where(odd, own_decay, other_decay)
    total_state = second_decay[:, None, None] * first_state + jnp.where(
        odd, own_state, other_state
    )
    total_decay = first_decay * second_decay
    before, before_decay = jnp.zeros_like(first_state), jnp.ones_like(first_decay)
    stride = 2
    while stride < size:
        later = (lax.axis_index(axis) & stride) != 0
        came = lax.ppermute(
            packed(total_state, total_decay), axis, [(i, i ^ stride) for i in range(size)]
        )
        came_state, came_decay = unpacked(came, half)
        before = jnp.where(later, before_decay[:, None, None] * came_state + before, before)
        before_decay = jnp.where(later, before_decay * came_decay, before_decay)
        early_state = jnp.where(later, came_state, total_state)
        late_state = jnp.where(later, total_state, came_state)
        late_decay = jnp.where(later, total_decay, came_decay)
        total_state = late_decay[:, None, None] * early_state + late_state
        total_decay = total_decay * came_decay
        stride *= 2
    inner = first_decay[:, None, None] * before + first_state
    mine_half = jnp.where(odd, inner, before)
    send_half = jnp.where(odd, before, inner).astype(jnp.bfloat16)
    back = lax.ppermute(
        send_half.reshape(-1, STATE), axis, [(i, i ^ 1) for i in range(size)]
    )
    back = back.astype(jnp.float32).reshape(mine_half.shape)
    low = jnp.where(odd, back, mine_half)
    high = jnp.where(odd, mine_half, back)
    return jnp.concatenate([low, high], axis=0)


def ring_step(parts, axis, step):
    size = lax.axis_size(axis)
    order = seq_ring(size)
    ahead, behind = parts
    last = 2 * step >= size
    first = [shift(ahead[0], axis, order, 1)] + ([] if last else [shift(behind[0], axis, order, -1)])
    second = [shift(behind[1], axis, order, -1)] + ([] if last else [shift(ahead[1], axis, order, 1)])
    if last:
        return (first[0],), (second[0],)
    return (first[0], second[1]), (first[1], second[0])


def head_scatter(pieces, axis):
    size, mine = lax.axis_size(axis), lax.axis_index(axis)
    stride = 1
    while stride < size:
        bit = (mine & stride) != 0
        bit = bit.astype(jnp.int32)
        left = pieces.shape[0] // 2
        view = pieces.reshape(left, 2, *pieces.shape[1:])
        send = lax.dynamic_index_in_dim(
            view, 1 - bit, 1, keepdims=False, allow_negative_indices=False
        )
        keep = lax.dynamic_index_in_dim(
            view, bit, 1, keepdims=False, allow_negative_indices=False
        )
        came = lax.ppermute(send, axis, [(i, i ^ stride) for i in range(size)])
        pieces = (keep.astype(jnp.float32) + came.astype(jnp.float32)).astype(jnp.bfloat16)
        stride *= 2
    return pieces[0]


def across(x, mask):
    axes = ("seq", "head")
    return lax.ppermute(x, axes, [(i, i ^ mask) for i in range(lax.axis_size(axes))])


def expert_half(slot_rows, up_weight, down_weight):
    model_width = slot_rows.shape[-1]
    flat_rows = slot_rows.reshape(-1, model_width)
    activation = jnp.dot(flat_rows, up_weight[0], preferred_element_type=jnp.float32)
    activation = jnp.maximum(activation, 0.0)
    activation = (activation * activation).astype(jnp.bfloat16)
    output = jnp.dot(activation, down_weight[0], preferred_element_type=jnp.float32).astype(
        jnp.bfloat16
    )
    return output.reshape(slot_rows.shape)


def per_device(
    ssm_values,
    ssm_gate,
    write_proj,
    read_proj,
    step_size,
    decay_power,
    skip_gain,
    norm_gain,
    out_weight,
    residual,
    expert_norm,
    router_weight,
    expert_index,
    up_weight,
    down_weight,
):
    tokens_dev = ssm_values.shape[0]
    heads_dev = step_size.shape[1]
    per_group = HEADS // GROUPS
    groups_dev = heads_dev // per_group
    count_blocks = tokens_dev // BLOCK_LEN
    seq_size = lax.axis_size("seq")
    head_size = lax.axis_size("head")
    shard = out_weight.T
    cut = (shard.shape[0] // 2 + 15) // 16 * 16
    halves = (shard[:cut], shard[cut:])
    ring = [ring_step((halves, halves), "seq", 1)]
    decay_rates = jnp.exp2(-decay_power.astype(jnp.float32))
    values = ssm_values.reshape(count_blocks, BLOCK_LEN, heads_dev, HEAD_DIM)
    steps_all = step_size.reshape(count_blocks, BLOCK_LEN, heads_dev)
    writes = write_proj.reshape(count_blocks, BLOCK_LEN, groups_dev, STATE)
    reads = read_proj.reshape(count_blocks, BLOCK_LEN, groups_dev, STATE)
    causal = jnp.tril(jnp.ones((BLOCK_LEN, BLOCK_LEN), dtype=bool))

    def one_block(pieces):
        values_in, steps_in, write_in, read_in = pieces
        log_decay = -steps_in * decay_rates[None, :]
        cumulative = jnp.cumsum(log_decay, axis=0)
        scores = jnp.einsum(
            "tgn,sgn->gts", read_in, write_in, preferred_element_type=jnp.float32
        )
        scores = jnp.repeat(scores, per_group, axis=0)
        decays = jnp.exp(cumulative.T[:, :, None] - cumulative.T[:, None, :])
        mixing = jnp.where(causal[None], scores * decays * steps_in.T[:, None, :], 0.0).astype(
            jnp.bfloat16
        )
        inner_out = jnp.einsum(
            "hts,shp->thp", mixing, values_in, preferred_element_type=jnp.float32
        )
        block_total = cumulative[-1]
        weighted = (
            values_in.astype(jnp.float32)
            * (jnp.exp(block_total[None, :] - cumulative) * steps_in)[:, :, None]
        ).astype(jnp.bfloat16)
        write_heads = jnp.repeat(write_in, per_group, axis=1)
        fresh_state = jnp.einsum(
            "shp,shn->hpn", weighted, write_heads, preferred_element_type=jnp.float32
        )
        return (inner_out, fresh_state, block_total, cumulative)

    inner_all, fresh_all, totals_blk, cumul_all = lax.map(
        one_block, (values, steps_all, writes, reads)
    )

    def summarize(carried_in, pieces):
        decay_prod, summary = carried_in
        block_total, fresh_state = pieces
        factor = jnp.exp(block_total)
        return ((decay_prod * factor, factor[:, None, None] * summary + fresh_state), None)

    zero_state = jnp.zeros((heads_dev, HEAD_DIM, STATE), jnp.float32)
    (device_decay, device_state), unused = lax.scan(
        summarize, (jnp.ones((heads_dev,), jnp.float32), zero_state), (totals_blk, fresh_all)
    )

    got = swapped(device_decay, device_state, "seq")
    for step in range(2, seq_size // 2 + 1):
        ring.append(ring_step(ring[-1], "seq", step))
    incoming = entering(got, device_decay, device_state, "seq")

    def emit_rows(carry_state, pieces):
        read_in, cumulative, block_total, fresh_state = pieces
        read_heads = jnp.repeat(read_in, per_group, axis=1)
        carried = jnp.einsum(
            "thn,hpn->thp",
            read_heads,
            carry_state.astype(jnp.bfloat16),
            preferred_element_type=jnp.float32,
        )
        carried = carried * jnp.exp(cumulative)[:, :, None]
        return (jnp.exp(block_total)[:, None, None] * carry_state + fresh_state, carried)

    _, carried_all = lax.scan(
        emit_rows, incoming, (reads, cumul_all, totals_blk, fresh_all)
    )
    values_flat = ssm_values.reshape(tokens_dev, heads_dev, HEAD_DIM).astype(jnp.float32)
    ssm_out = (inner_all + carried_all).reshape(tokens_dev, heads_dev, HEAD_DIM) + skip_gain[
        None, :, None
    ] * values_flat
    gate_vals = ssm_gate.reshape(tokens_dev, heads_dev, HEAD_DIM).astype(jnp.float32)
    gated = (ssm_out * jax.nn.silu(gate_vals)).reshape(tokens_dev, groups_dev, per_group * HEAD_DIM)
    inv_rms = lax.rsqrt(jnp.mean(gated * gated, axis=-1, keepdims=True) + EPSILON)
    normed = (
        (gated * inv_rms).reshape(tokens_dev, heads_dev * HEAD_DIM) * norm_gain[None, :]
    ).astype(jnp.bfloat16)
    rows_own = tokens_dev // head_size
    shard_width = out_weight.shape[1]

    def product(parts):
        rows = parts[0] if len(parts) == 1 else jnp.concatenate(parts, axis=0)
        result = lax.dot_general(
            normed, rows, (((1,), (1,)), ((), ())), preferred_element_type=jnp.float32
        ).astype(jnp.bfloat16)
        return [
            result[:, at : at + shard_width].reshape(head_size, 1, rows_own, shard_width)
            for at in range(0, result.shape[1], shard_width)
        ]

    offsets, products = [0], product([shard])
    batches = []
    for step in range(1, seq_size // 2 + 1):
        ahead, behind = ring[step - 1]
        offsets += [-step, step] if 2 * step < seq_size else [-step]
        products += product([*ahead, *behind])
        if step in (seq_size // 4, seq_size // 2 - 1, seq_size // 2):
            batches.append(head_scatter(jnp.concatenate(products, axis=1), "head"))
            products = []
    scattered = jnp.concatenate(batches, axis=0)
    came = {step % seq_size: at for at, step in enumerate(offsets)}
    in_order = jnp.concatenate([scattered[came[step] : came[step] + 1] for step in range(seq_size)] * 2, axis=0)
    index = lax.axis_index("seq")
    ring_place = jnp.where((index & 1) == 0, index >> 1, seq_size - 1 - (index >> 1))
    on_ring = lax.dynamic_slice_in_dim(
        in_order, seq_size - ring_place, seq_size, allow_negative_indices=False
    )
    order = seq_ring(seq_size)
    mixed_out = jnp.concatenate(
        [on_ring[order.index(b)] for b in range(seq_size)], axis=1
    ).astype(jnp.float32)
    hidden = residual.astype(jnp.float32) + mixed_out
    inputs = (
        hidden
        * lax.rsqrt(jnp.mean(hidden * hidden, axis=-1, keepdims=True) + EPSILON)
        * expert_norm[None, :]
    ).astype(jnp.bfloat16)
    logits = jnp.dot(inputs, router_weight, preferred_element_type=jnp.float32)
    experts = router_weight.shape[1]
    model_width = inputs.shape[1]
    expert_hits = (
        expert_index[:, :, None] == jnp.arange(experts, dtype=jnp.int32)[None, None, :]
    )
    picked = jnp.sum(jnp.where(expert_hits, logits[:, None, :], 0.0), axis=-1)
    probability = jax.nn.sigmoid(picked)
    shares = ROUTE_SCALE * probability / jnp.sum(probability, axis=1, keepdims=True)
    flat_hits = expert_hits.astype(jnp.int32).reshape(rows_own * TOP, experts)
    before = jnp.cumsum(flat_hits, axis=0) - flat_hits
    slot_index = jnp.sum(before * flat_hits, axis=1).reshape(rows_own, TOP)
    capacity = 8 * TOP * tokens_dev // (3 * seq_size * head_size * head_size)
    notes = jnp.concatenate(
        [expert_index.astype(jnp.bfloat16), slot_index.astype(jnp.bfloat16), shares.astype(jnp.bfloat16)],
        axis=1,
    )
    notes = jnp.pad(notes, ((0, 0), (0, 128 - notes.shape[1])))
    moe_out = routed(
        jnp.concatenate([inputs, notes], axis=1), model_width, capacity, experts, up_weight, down_weight
    )
    return (hidden + moe_out).astype(jnp.bfloat16)


def routed(block, width, capacity, experts, up_weight, down_weight):
    inner = experts // 4
    stride = 2 * inner
    place = lax.axis_index("seq") * lax.axis_size("head") + lax.axis_index("head")
    mine_inner = (place >> 1) & (inner - 1)
    turned = mine_inner ^ jnp.arange(inner, dtype=jnp.int32)
    wanted = ((place >> 1) - mine_inner + turned)[:, None] * capacity + jnp.arange(capacity, dtype=jnp.int32)
    wanted = wanted.reshape(-1).astype(jnp.float32)

    turns = (0, 2, 3, 1)

    def placed(rows):
        notes = rows[:, width : width + 3 * TOP].astype(jnp.float32)
        code = notes[:, :TOP] * capacity + notes[:, TOP : 2 * TOP]
        match = code[:, :, None] == wanted[None, None, :]
        placing = jnp.any(match, axis=1).astype(jnp.bfloat16)
        weights = jnp.sum(jnp.where(match, notes[:, 2 * TOP :, None], 0.0), axis=1)
        return placing, weights.astype(jnp.bfloat16)

    def spread(rows, summed=None):
        placing, weights = placed(rows)
        inputs = rows[:, :width]
        parts, results = [], []
        for m in range(inner):
            here = slice(m * capacity, (m + 1) * capacity)
            part = lax.dot_general(
                placing[:, here],
                inputs,
                (((0,), (0,)), ((), ())),
                preferred_element_type=jnp.float32,
            ).astype(jnp.bfloat16)
            result = None if summed is None else summed[here]
            if m:
                both = part if summed is None else jnp.concatenate([part, result], axis=0)
                both = across(both, 2 * m)
                part, result = both[:capacity], both[capacity:]
            parts.append(part)
            results.append(result)
        return parts, weights, results

    def expert(parts):
        own_rows = jnp.concatenate(parts, axis=0)
        other_rows = across(own_rows, 1)
        rows = jnp.concatenate([own_rows, other_rows], axis=0)
        both = expert_half(rows, up_weight, down_weight)
        half = own_rows.shape[0]
        back = across(both[half:], 1)
        return (both[:half].astype(jnp.float32) + back.astype(jnp.float32)).astype(jnp.bfloat16)

    def brought(summed):
        results = []
        for m in range(inner):
            part = summed[m * capacity : (m + 1) * capacity]
            results.append(across(part, 2 * m) if m else part)
        return results

    def home(results, weights, k):
        partial = jnp.dot(
            weights, jnp.concatenate(results, axis=0), preferred_element_type=jnp.float32
        )
        return across(partial.astype(jnp.bfloat16), turns[k] * stride) if k else partial

    def line(k):
        return across(block, turns[k] * stride)

    rows1 = line(1)
    sent0 = spread(block)
    rows1, sent0, block = lax.optimization_barrier((rows1, sent0[:2], block))

    rows2 = line(2)
    sent1 = spread(rows1)
    done0 = expert(sent0[0])
    rows2, sent1, done0, block = lax.optimization_barrier((rows2, sent1[:2], done0, block))

    rows3 = line(3)
    sent2 = spread(rows2, done0)
    done1 = expert(sent1[0])
    rows3, sent2, done1 = lax.optimization_barrier((rows3, sent2, done1))

    sent3 = spread(rows3, done1)
    done2 = expert(sent2[0])
    sum0 = home(sent2[2], sent0[1], 0)
    sent3, done2, sum0 = lax.optimization_barrier((sent3, done2, sum0))

    done3 = expert(sent3[0])
    back2 = brought(done2)
    sum1 = home(sent3[2], sent1[1], 1)
    back3 = brought(done3)
    sum2 = home(back2, sent2[1], 2)
    sum3 = home(back3, sent3[1], 3)
    total = sum0
    for part in (sum1, sum2, sum3):
        total = total + part.astype(jnp.float32)
    return total


def solution(mesh):
    return jax.shard_map(
        per_device,
        mesh=mesh,
        in_specs=(
            P(("grp", "seq"), "head"),
            P(("grp", "seq"), "head"),
            P(("grp", "seq"), "head"),
            P(("grp", "seq"), "head"),
            P(("grp", "seq"), "head"),
            P("head"),
            P("head"),
            P("head"),
            P("head", "seq"),
            P(("grp", "seq", "head"), None),
            P(),
            P(),
            P(("grp", "seq", "head"), None),
            P(("seq", "head"), None, None),
            P(("seq", "head"), None, None),
        ),
        out_specs=P(("grp", "seq", "head"), None),
        check_vma=False,
    )
```
